128 devices in a mesh: section: 8 (over z, x_lo), dp: 16 (over y, x_hi, core).
Axes of the slice: x: 4 (x_hi: 2, x_lo: 2; x = x_hi * 2 + x_lo), y: 4, z: 4, core: 2. Of those that a mesh axis runs over, the one named last changes fastest.
Arguments:
- master: float32 [8, 2560, 2560], P('section', 'dp'), may hold values from -0.125 to 0.125
- first_moment: float32 [8, 2560, 2560], P('section', 'dp'), may hold values from -3 to 3
- second_moment: float32 [8, 2560, 2560], P('section', 'dp'), may hold values from 0.1 to 4
- inputs_own: bfloat16 [8, 4, 2048, 2560], P('section', None, 'dp'), may hold values from -6 to 6
- inputs_arriving: bfloat16 [8, 4, 2048, 2560], P('section', None, 'dp'), may hold values from -6 to 6
- grads_own: bfloat16 [8, 4, 2048, 2560], P('section', None, 'dp'), may hold values from -0.13183594 to 0.13183594
- windows_own: int32 [8, 2048, 2560], P('section', 'dp'), may hold values from 0 to 15
- windows_arriving: int32 [8, 2048, 2560], P('section', 'dp'), may hold values from 0 to 15
- next_inputs: bfloat16 [8, 512, 2560], P('section', 'dp'), may hold values from -6 to 6
Outputs:
- fresh_params: float32 [8, 2560, 2560], P('section', 'dp')
- fresh_first: float32 [8, 2560, 2560], P('section', 'dp')
- fresh_second: float32 [8, 2560, 2560], P('section', 'dp')
- next_currents: bfloat16 [8, 512, 2560], P('section', 'dp')
The draws below stay inside these ranges and needn't reach their ends.
Inputs may be any that keep to these rules, and one draw needn't show every extreme that they name: `windows_own`: bit t of an entry is the surrogate derivative of spikes_t by v_t for timestep t. `windows_arriving`: bit t of an entry is the surrogate derivative of spikes_t by v_t for timestep t.
All inputs are finite; a program needn't handle non-finite values.
Results may differ from the reference program's by a relative error of at most 0.008.
Values may be sent and summed in bfloat16 or wider, within the bound.
A program may use at most 128 MiB of HBM per device.

```python
import math
import jax
import jax.numpy as jnp
from jax import lax

FEATURES = 2560
TIMESTEPS = 4
TOK_DEV = 128
SECTIONS = 8
TOKENS = 2048
NEXT_TOKENS = 512
N_DP = 16


def touch_ends(entries, key, low, high):
    longest = entries.shape.index(max(entries.shape))
    spots = []
    for shift in (0, 1):
        where = [jax.random.randint(jax.random.fold_in(key, axis), (), 0, length) for axis, length in enumerate(entries.shape)]
        where[longest] = (where[longest] + shift) % entries.shape[longest]
        spots.append(tuple(where))
    return entries.at[spots[0]].set(low).at[spots[1]].set(high)


def shard_levels(key, dims, split, smallest, high):
    def one(position, shards_of):
        steps = jax.random.uniform(jax.random.fold_in(jax.random.fold_in(key, 6), position), (shards_of,), jnp.float32, smallest / len(split), high / len(split))
        return jnp.repeat(jnp.exp(steps), dims[position] // shards_of).reshape((-1,) + (1,) * (len(dims) - position - 1))

    level = one(*split[0])
    for cut in split[1:]:
        level = level * one(*cut)
    return level


def bell_draw(key, extent, scale, most, shards=(), held_as=jnp.bfloat16):
    loudness = shard_levels(key, extent, shards, -0.22, 0.18) if shards else 1.0
    drawn = jax.random.normal(key, extent, jnp.float32) * scale * loudness
    return jnp.minimum(jnp.maximum(drawn, -most), most).astype(held_as)


def setup_inputs(seed: int = 0) -> dict:
    streams_of = jax.random.split(jax.random.key(seed), 10)
    return {
        "master": bell_draw(streams_of[0], (SECTIONS, FEATURES, FEATURES), FEATURES ** -0.5, 0.125, ((0, 8), (1, 16)), jnp.float32),
        "first_moment": bell_draw(streams_of[1], (SECTIONS, FEATURES, FEATURES), 0.5, 3.0, ((0, 8), (1, 16)), jnp.float32),
        "second_moment": jnp.clip(jnp.exp(math.log(4.0) - 3.6888794 * jax.random.uniform(streams_of[2], (SECTIONS, FEATURES, FEATURES), jnp.float32) ** shard_levels(streams_of[2], (SECTIONS, FEATURES, FEATURES), ((0, 8), (1, 16)), -0.2, 0.2)), 0.1, 4.0),
        "inputs_own": bell_draw(streams_of[3], (SECTIONS, TIMESTEPS, TOKENS, FEATURES), 1.0, 6.0, ((0, 8), (2, 16))),
        "inputs_arriving": bell_draw(streams_of[4], (SECTIONS, TIMESTEPS, TOKENS, FEATURES), 1.0, 6.0, ((0, 8), (2, 16))),
        "grads_own": bell_draw(streams_of[5], (SECTIONS, TIMESTEPS, TOKENS, FEATURES), (2 * (TIMESTEPS * TOKENS) ** -0.5), 0.13183594, ((0, 8), (2, 16))),
        "windows_own": touch_ends(jax.random.randint(streams_of[6], (SECTIONS, TOKENS, FEATURES), 0, 2 ** TIMESTEPS), jax.random.fold_in(streams_of[6], 1), 0, (2 ** TIMESTEPS) - 1).astype(jnp.int32),
        "windows_arriving": touch_ends(jax.random.randint(streams_of[7], (SECTIONS, TOKENS, FEATURES), 0, 2 ** TIMESTEPS), jax.random.fold_in(streams_of[7], 1), 0, (2 ** TIMESTEPS) - 1).astype(jnp.int32),
        "next_inputs": bell_draw(streams_of[8], (SECTIONS, NEXT_TOKENS, FEATURES), 1.0, 6.0, ((0, 8), (1, 16))),
    }


LEAK_RATE = 0.5
LEARN_RATE = 0.002
FIRST_DECAY = 0.9
SECOND_DECAY = 0.95
EPSILON = 1e-08
WEIGHT_DECAY = 0.1
FIRST_CORRECTION = 1.0 - 0.9 ** 10
SECOND_CORRECTION = 1.0 - 0.95 ** 10

def membrane_grads(gradients, windows):
    carried = jnp.zeros(gradients.shape[1:], jnp.float32)
    results = []
    for moment in reversed(range(gradients.shape[0])):
        window = jnp.bitwise_and(jnp.right_shift(windows, moment), 1).astype(jnp.float32)
        carried = window * gradients[moment].astype(jnp.float32) + LEAK_RATE * carried
        results = [carried] + results
    return jnp.stack(results).astype(jnp.bfloat16)

def send_grad(bundle):
    params, gradients, windows = bundle
    membrane = membrane_grads(gradients, windows).reshape(TIMESTEPS * TOKENS, FEATURES)
    through = jnp.dot(membrane, params.astype(jnp.bfloat16).T, preferred_element_type=jnp.float32)
    summed = gradients.reshape(TIMESTEPS * TOKENS, FEATURES).astype(jnp.float32) + through
    return summed.astype(jnp.bfloat16).reshape(TIMESTEPS, TOKENS, FEATURES)

def update_section(bundle):
    params, first_old, second_old, acts_own, acts_arriving, grads_now, windows_now, received, windows_later, upcoming = bundle
    membrane_own = membrane_grads(grads_now, windows_now)
    membrane_arriving = membrane_grads(received, windows_later)

    def shard_term(shard_index, running):
        offset = (shard_index * TOK_DEV).astype(jnp.int32)

        def flatten_rows(values):
            return lax.dynamic_slice_in_dim(values, offset, TOK_DEV, 1).reshape(TIMESTEPS * TOK_DEV, FEATURES)
        partial_value = jnp.dot(flatten_rows(acts_own).T, flatten_rows(membrane_own), preferred_element_type=jnp.float32)
        partial_value = partial_value + jnp.dot(flatten_rows(acts_arriving).T, flatten_rows(membrane_arriving), preferred_element_type=jnp.float32)
        rounded = lax.optimization_barrier(partial_value.astype(jnp.bfloat16))
        return running + rounded.astype(jnp.float32)
    gradient = lax.fori_loop(0, N_DP, shard_term, jnp.zeros((FEATURES, FEATURES), jnp.float32))
    fresh_first = FIRST_DECAY * first_old + (1.0 - FIRST_DECAY) * gradient
    fresh_second = SECOND_DECAY * second_old + (1.0 - SECOND_DECAY) * gradient * gradient
    direction = fresh_first / FIRST_CORRECTION / (jnp.sqrt(fresh_second / SECOND_CORRECTION) + EPSILON)
    fresh_params = params - LEARN_RATE * (direction + WEIGHT_DECAY * params)
    product = jnp.dot(upcoming, fresh_params.astype(jnp.bfloat16), preferred_element_type=jnp.float32)
    return (fresh_params, fresh_first, fresh_second, product.astype(jnp.bfloat16))

def reference(master, first_moment, second_moment, inputs_own, inputs_arriving, grads_own, windows_own, windows_arriving, next_inputs):
    outgoing = lax.map(send_grad, (master, grads_own, windows_own))
    received = jnp.concatenate([outgoing[1:], jnp.zeros_like(outgoing[:1])], axis=0)
    fresh_params, fresh_first, fresh_second, next_currents = lax.map(update_section, (master, first_moment, second_moment, inputs_own, inputs_arriving, grads_own, windows_own, received, windows_arriving, next_inputs))
    return (fresh_params, fresh_first, fresh_second, next_currents)
```

```python
import jax
import jax.numpy as jnp
from jax import lax
from jax.experimental import pallas as pl
from jax.experimental.pallas import tpu as pltpu
from jax.sharding import PartitionSpec as P

LEAK_RATE = 0.5
LEARN_RATE = 0.002
FIRST_DECAY = 0.9
SECOND_DECAY = 0.95
EPSILON = 1e-08
WEIGHT_DECAY = 0.1
FIRST_CORRECTION = 1.0 - 0.9**10
SECOND_CORRECTION = 1.0 - 0.95**10

MESH = pl.DeviceIdType.MESH
F32, BF16 = jnp.float32, jnp.bfloat16
FEAT, HALF, QUART, OWN = 2560, 1280, 640, 160
ROWS, TOK, STEPS = 512, 128, 4
YW = 768
XW = HALF - YW


def al(value, by):
    return pl.multiple_of(value, by)


def kernel(
    master, first, second, xo, xa, grads, wo, wa, ni,
    out_p, out_m, out_v, out_c,
    wb, mo, mos, xov, xav, acc, gv, wov, wav, mst, outb, rcv, niw,
    r1, r23, rx, qx, q1, q23, gx, cz, cr, res,
    loc, snd, wr, ws, xs, nr, pr, rr, zr, cs,
):
    s, d = lax.axis_index("section"), lax.axis_index("dp")
    y, xh, c, k = d // 4, (d // 2) % 2, d % 2, d // 2
    yp, ym, y2 = (y + 1) % 4, (y + 3) % 4, (y + 2) % 4

    def index(y_, xh_, c_):
        return (y_ * 2 + xh_) * 2 + c_

    sib, xp = (s, index(y, xh, 1 - c)), (s, index(y, 1 - xh, c))
    up, down = (s, index(yp, xh, c)), (s, index(ym, xh, c))
    used = [0]

    def send(src, dst, sem, dev):
        copy = pltpu.make_async_remote_copy(
            src_ref=src, dst_ref=dst, send_sem=snd.at[used[0]], recv_sem=sem,
            device_id=dev, device_id_type=MESH,
        )
        used[0] += 1
        copy.start()
        return copy

    def arrived(dst, sem):
        pltpu.make_async_remote_copy(
            src_ref=dst, dst_ref=dst, send_sem=snd.at[0], recv_sem=sem,
            device_id=sib, device_id_type=MESH,
        ).wait_recv()

    def load(src, dst, i):
        copy = pltpu.make_async_copy(src, dst, loc.at[i])
        copy.start()
        return copy

    def owner(y_, xh_, c_, part=0, rows=OWN):
        return wb.at[pl.ds(al(index(y_, xh_, c_) * OWN + part, 16), rows)]

    def half(which):
        return pl.ds(al(which * HALF, 128), HALF)

    l_mst = load(master, mst, 0)
    l_g = load(grads, gv, 1)
    l_wo = load(wo, wov, 2)
    l_xo = load(xo, xov.at[c], 3)
    l_xa = load(xa, xav.at[c], 4)
    l_wa = load(wa.at[:, half(c)], wav.at[c], 5)

    def base(e):
        return al(e * OWN - (e % 4) * 32, 128)

    l_ni = load(
        ni.at[:, pl.ds(base(d), 256)], niw.at[pl.ds(al(c * 256 + k * 32, 32), 32)], 6
    )

    barrier = pltpu.get_barrier_semaphore()
    for i in range(1, 16):
        pl.semaphore_signal(barrier, inc=1, device_id=(s, (d + i) % 16), device_id_type=MESH)

    @pl.when(s > 0)
    def _():
        for h in range(2):
            pl.semaphore_signal(barrier, inc=1, device_id=(s - 1, k * 2 + h), device_id_type=MESH)

    @pl.when(s < 7)
    def _():
        for h in range(2):
            pl.semaphore_signal(barrier, inc=1, device_id=(s + 1, k * 2 + h), device_id_type=MESH)

    l_mst.wait()

    @pl.loop(0, OWN // 16)
    def _(r):
        wb[pl.ds(al(d * OWN + r * 16, 16), 16), :] = mst[pl.ds(al(r * 16, 16), 16), :].astype(BF16)

    pl.semaphore_wait(barrier, 15 + 2 * jnp.minimum(s, 1) + 2 * jnp.minimum(7 - s, 1))

    mine = owner(y, xh, c)
    w_sends = [
        send(mine, mine, wr.at[0], xp),
        send(mine, mine, wr.at[1], up),
        send(mine, mine, wr.at[2], down),
        send(mine, mine, ws.at[0], sib),
    ]
    x_sends = [
        send(xo, xov.at[c], xs.at[0], sib),
        send(wa.at[:, half(1 - c)], wav.at[c], xs.at[1], sib),
        send(xa, xav.at[c], xs.at[2], sib),
    ]
    n_sends = []
    for i in range(1, 16):
        e = (d + i) % 16
        n_sends.append(
            send(
                ni.at[:, pl.ds(base(e), 256)],
                niw.at[pl.ds(al(c * 256 + k * 32, 32), 32)],
                nr.at[i],
                (s, e),
            )
        )

    l_g.wait()
    l_wo.wait()

    @pl.loop(0, TOK // 16)
    def _(r):
        for q in range(4):
            cols = pl.ds(q * QUART, QUART)
            bits = wov[pl.ds(al(r * 16, 16), 16), cols]
            carry = jnp.zeros((16, QUART), F32)
            for t in reversed(range(STEPS)):
                rows = pl.ds(al(t * TOK + r * 16, 16), 16)
                window = ((bits >> t) & 1).astype(F32)
                carry = window * gv[rows, cols].astype(F32) + LEAK_RATE * carry
                mo[rows, cols] = carry.astype(BF16)

    x_sends.append(send(mo.at[:, half(1 - c)], mos, xs.at[3], sib))

    across = (((0,), (0,)), ((), ()))
    l_xo.wait()
    arrived(xov.at[1 - c], xs.at[0])
    arrived(mos, xs.at[3])

    @pl.loop(0, 4)
    def _(b):
        rows = pl.ds(al(b * QUART, 128), QUART)
        for j in range(2):
            acc[rows, pl.ds(j * QUART, QUART)] = lax.dot_general(
                xov[c, :, rows],
                mo[:, pl.ds(al(c * HALF + j * QUART, 128), QUART)],
                across,
                preferred_element_type=F32,
            ) + lax.dot_general(
                xov[1 - c, :, rows],
                mos[:, pl.ds(j * QUART, QUART)],
                across,
                preferred_element_type=F32,
            )

    p_sends = []

    def outgoing(b, n):
        cols = pl.ds(al(b * QUART, 128), QUART)
        for h in (1, 0):
            rows = pl.ds(h * 256, 256)
            through = lax.dot_general(
                mo[rows, :], wb[cols, :], (((1,), (1,)), ((), ())), preferred_element_type=F32
            )
            outb[n, rows, :] = (gv[rows, cols].astype(F32) + through).astype(BF16)

            copy = pltpu.make_async_remote_copy(
                src_ref=outb.at[n, rows],
                dst_ref=rcv.at[c, b % 2, rows],
                send_sem=snd.at[used[0]],
                recv_sem=pr.at[c, b % 2, h],
                device_id=(s - 1, k * 2 + b // 2),
                device_id_type=MESH,
            )
            used[0] += 1
            p_sends.append(copy)
            pl.when(s > 0)(copy.start)

    def relay(kind, piece, *targets):
        arrived(piece, wr.at[kind])
        for region, sem, dev in targets:
            w_sends.append(send(region, region, sem, dev))

    piece = owner(y, 1 - xh, c)
    relay(0, piece, (piece, wr.at[3], up), (piece, wr.at[4], down), (piece, ws.at[1], sib))
    piece = owner(ym, xh, c)
    relay(1, piece, (owner(ym, xh, c, 0, 80), wr.at[5], up), (piece, ws.at[2], sib))
    piece = owner(yp, xh, c)
    relay(2, piece, (owner(yp, xh, c, 80, 80), wr.at[6], down), (piece, ws.at[3], sib))
    arrived(owner(y, xh, 1 - c), ws.at[0])
    arrived(owner(y, 1 - xh, 1 - c), ws.at[1])
    outgoing(y, 0)
    piece = owner(ym, 1 - xh, c)
    relay(3, piece, (owner(ym, 1 - xh, c, 0, 80), wr.at[7], up), (piece, ws.at[4], sib))
    piece = owner(yp, 1 - xh, c)
    relay(4, piece, (owner(yp, 1 - xh, c, 80, 80), wr.at[8], down), (piece, ws.at[5], sib))
    arrived(owner(ym, xh, 1 - c), ws.at[2])
    arrived(owner(ym, 1 - xh, 1 - c), ws.at[4])
    outgoing(ym, 1)
    arrived(owner(yp, xh, 1 - c), ws.at[3])
    arrived(owner(yp, 1 - xh, 1 - c), ws.at[5])
    outgoing(yp, 2)
    for i, (xh_, part) in enumerate(((xh, 0), (xh, 80), (1 - xh, 0), (1 - xh, 80))):
        piece = owner(y2, xh_, c, part, 80)
        relay(5 + i, piece, (piece, ws.at[6 + i], sib))
    for i, (xh_, part) in enumerate(((xh, 0), (xh, 80), (1 - xh, 0), (1 - xh, 80))):
        arrived(owner(y2, xh_, 1 - c, part, 80), ws.at[6 + i])
    outgoing(y2, 3)

    def far(b):
        away = (b - y + 4) % 4
        return jnp.minimum(away, 4 - away)

    early = jnp.where(far(2 * c) < far(2 * c + 1), 0, 1)
    late = 1 - early
    l_xa.wait()
    arrived(xav.at[1 - c], xs.at[2])
    l_wa.wait()
    arrived(wav.at[1 - c], xs.at[1])

    def arriving(j):
        for cc in range(2):
            for h in (1, 0):
                arrived(rcv.at[cc, j, pl.ds(h * 256, 256)], pr.at[cc, j, h])

            @pl.loop(0, TOK // 16)
            def _(r, cc=cc):
                bits = wav[cc, pl.ds(al(r * 16, 16), 16), pl.ds(al(j * QUART, 128), QUART)]
                carry = jnp.zeros((16, QUART), F32)
                for t in reversed(range(STEPS)):
                    rows = pl.ds(al(t * TOK + r * 16, 16), 16)
                    window = ((bits >> t) & 1).astype(F32)
                    carry = window * rcv[cc, j, rows, :].astype(F32) + LEAK_RATE * carry
                    rcv[cc, j, rows, :] = carry.astype(BF16)

    def more(b, j):
        rows = pl.ds(al(b * QUART, 128), QUART)
        cols = pl.ds(al(j * QUART, 128), QUART)
        acc[rows, cols] += lax.dot_general(
            xav[0, :, rows], rcv[0, j], across, preferred_element_type=F32
        ) + lax.dot_general(xav[1, :, rows], rcv[1, j], across, preferred_element_type=F32)

    @pl.when(s < 7)
    def _():
        arriving(early)

        @pl.loop(0, 4)
        def _(b):
            more(b, early)

        arriving(late)

    for copy in w_sends + x_sends:
        copy.wait_send()

    def unit(y_, xh_, n=2, first_=0):
        return pl.ds(al((y_ * 2 + xh_) * 2 * OWN + first_ * OWN, 32), n * OWN)

    def rounded(b):
        @pl.loop(0, QUART // 32)
        def _(r):
            rows = pl.ds(al(b * QUART + r * 32, 32), 32)
            wb[rows, pl.ds(0, HALF)] = acc[rows, :].astype(BF16)

    def finish(b):
        @pl.when(s < 7)
        def _():
            more(b, late)

        rounded(b)

    ycol, xcol = pl.ds(0, YW), pl.ds(YW, XW)
    r_sends = []

    def to_partner(b, n):
        r_sends.append(send(wb.at[unit(b, 1 - xh), xcol], qx.at[n], rr.at[7 + n], xp))

    finish(y2)
    r_sends.append(send(wb.at[unit(y2, 0), ycol], r1.at[0], rr.at[0], up))
    r_sends.append(send(wb.at[unit(y2, 1), ycol], r1.at[1], rr.at[1], down))
    to_partner(y2, 0)
    finish(yp)
    r_sends.append(send(wb.at[unit(yp, 1), ycol], r23.at[0, 1], rr.at[3], up))
    to_partner(yp, 1)
    finish(ym)
    r_sends.append(send(wb.at[unit(ym, 0), ycol], r23.at[1, 0], rr.at[4], down))
    to_partner(ym, 2)
    finish(y)
    to_partner(y, 3)

    def add(start, count, cols, *terms, to=None, keep=False):
        @pl.loop(0, count // 32)
        def _(r):
            rows = pl.ds(al(start + r * 32, 32), 32)
            total = acc[rows, cols]
            for term in terms:
                total += term[pl.ds(al(r * 32, 32), 32), :].astype(F32)
            if keep:
                acc[rows, cols] = total
            else:
                wb[rows, cols] = total.astype(BF16)

    def at_unit(y_, xh_, c_=0):
        return index(y_, xh_, c_) * OWN

    arrived(r1.at[0], rr.at[0])
    add(at_unit(yp, 0), 2 * OWN, ycol, r1.at[0])
    r_sends.append(send(wb.at[unit(yp, 0), ycol], r23.at[0, 0], rr.at[2], up))
    arrived(r1.at[1], rr.at[1])
    add(at_unit(ym, 1), 2 * OWN, ycol, r1.at[1])
    r_sends.append(send(wb.at[unit(ym, 1), ycol], r23.at[1, 1], rr.at[5], down))

    arrived(qx.at[0], rr.at[7])
    add(at_unit(y2, xh), 2 * OWN, xcol, qx.at[0])
    r_sends.append(send(wb.at[unit(y2, xh, 1, 0), xcol], q1.at[0], rr.at[11], up))
    r_sends.append(send(wb.at[unit(y2, xh, 1, 1), xcol], q1.at[1], rr.at[12], down))
    arrived(qx.at[1], rr.at[8])
    add(at_unit(yp, xh, 1), OWN, xcol, qx.at[1, pl.ds(OWN, OWN)])
    r_sends.append(send(wb.at[unit(yp, xh, 1, 1), xcol], q23.at[0, 1], rr.at[14], up))
    add(at_unit(yp, xh, 0), OWN, xcol, qx.at[1, pl.ds(0, OWN)], keep=True)
    arrived(qx.at[2], rr.at[9])
    add(at_unit(ym, xh, 0), OWN, xcol, qx.at[2, pl.ds(0, OWN)])
    r_sends.append(send(wb.at[unit(ym, xh, 1, 0), xcol], q23.at[1, 0], rr.at[15], down))
    add(at_unit(ym, xh, 1), OWN, xcol, qx.at[2, pl.ds(OWN, OWN)], keep=True)
    l_m = [load(first.at[:, half(h)], acc.at[unit(y2, h, 1, 0)], 7 + h) for h in range(2)]
    l_v = [load(second.at[:, half(h)], acc.at[unit(y2, h, 1, 1)], 9 + h) for h in range(2)]

    arrived(r23.at[0, 1], rr.at[3])
    arrived(r23.at[1, 0], rr.at[4])
    arrived(r23.at[0, 0], rr.at[2])
    arrived(r23.at[1, 1], rr.at[5])
    arrived(qx.at[3], rr.at[10])
    add(at_unit(y, 1 - xh), 2 * OWN, ycol, r23.at[0, 1 - xh], r23.at[1, 1 - xh])
    r_sends.append(send(wb.at[unit(y, 1 - xh), ycol], rx, rr.at[6], xp))
    add(at_unit(y, xh), 2 * OWN, ycol, r23.at[0, xh], r23.at[1, xh], keep=True)

    arrived(q1.at[0], rr.at[11])
    add(at_unit(yp, xh, 0), OWN, xcol, q1.at[0])
    r_sends.append(send(wb.at[unit(yp, xh, 1, 0), xcol], q23.at[0, 0], rr.at[13], up))
    arrived(q1.at[1], rr.at[12])
    add(at_unit(ym, xh, 1), OWN, xcol, q1.at[1])
    r_sends.append(send(wb.at[unit(ym, xh, 1, 1), xcol], q23.at[1, 1], rr.at[16], down))
    for u in range(2):
        arrived(q23.at[0, 1 - u], rr.at[13 + (1 - u)])
        arrived(q23.at[1, u], rr.at[15 + u])
    for u in range(2):
        add(
            at_unit(y, xh, u), OWN, xcol,
            qx.at[3, pl.ds(u * OWN, OWN)], q23.at[0, u], q23.at[1, u], keep=True,
        )
    arrived(rx, rr.at[6])
    add(at_unit(y, xh), 2 * OWN, ycol, rx, keep=True)

    r_sends.append(send(acc.at[pl.ds(al(at_unit(y, xh, 1 - c), 32), OWN)], gx, rr.at[17], sib))

    @pl.loop(0, 256 // 32)
    def _(r):
        mo[pl.ds(al(r * 32, 32), 32), :] = jnp.zeros((32, FEAT), BF16)

    for copy in l_m + l_v:
        copy.wait()
    shift = (d % 4) * 32
    stores = []

    def adam(which, gradient, start):
        @pl.loop(0, OWN // 16)
        def _(r):
            here = pl.ds(al(r * 16, 16), 16)
            cols = half(which)
            at_m = pl.ds(al(at_unit(y2, which, 0) + r * 16, 16), 16)
            at_v = pl.ds(al(at_unit(y2, which, 1) + r * 16, 16), 16)
            g = gradient[pl.ds(al(start + r * 16, 16), 16), :]
            params = mst[here, cols]
            m = FIRST_DECAY * acc[at_m, :] + (1.0 - FIRST_DECAY) * g
            v = SECOND_DECAY * acc[at_v, :] + (1.0 - SECOND_DECAY) * g * g
            acc[at_m, :] = m
            acc[at_v, :] = v
            direction = m / FIRST_CORRECTION / (jnp.sqrt(v / SECOND_CORRECTION) + EPSILON)
            new = params - LEARN_RATE * (direction + WEIGHT_DECAY * params)
            mst[here, cols] = new
            mo[pl.ds(al(shift + r * 16, 16), 16), cols] = new.astype(BF16)

        n = 11 if which is c else 14
        stores.append(load(mst.at[:, half(which)], out_p.at[:, half(which)], n))
        stores.append(load(acc.at[unit(y2, which, 1, 0)], out_m.at[:, half(which)], n + 1))
        stores.append(load(acc.at[unit(y2, which, 1, 1)], out_v.at[:, half(which)], n + 2))

    adam(c, acc, at_unit(y, xh, c))
    arrived(gx, rr.at[17])
    adam(1 - c, gx, 0)

    l_ni.wait()
    for i in range(1, 16):
        e = (d - i + 16) % 16
        arrived(niw.at[pl.ds(al((e % 2) * 256 + (e // 2) * 32, 32), 32)], nr.at[i])
    c_sends = []
    for q in range(4):
        cols = pl.ds(q * QUART, QUART)
        gv[pl.ds(0, 256), cols] = jnp.dot(
            niw[pl.ds(al((1 - c) * 256, 256), 256), :],
            mo[pl.ds(0, 256), cols],
            preferred_element_type=F32,
        ).astype(BF16)
        c_sends.append(send(gv.at[pl.ds(0, 256), cols], cz.at[:, cols], zr.at[q], sib))
    for q in range(4):
        cols = pl.ds(q * QUART, QUART)
        total = jnp.dot(
            niw[pl.ds(al(c * 256, 256), 256), :],
            mo[pl.ds(0, 256), cols],
            preferred_element_type=F32,
        )
        arrived(cz.at[:, cols], zr.at[q])
        gv[pl.ds(256, 256), cols] = (total + cz[:, cols].astype(F32)).astype(BF16)
    for i in range(1, 8):
        e = (k + i) % 8
        c_sends.append(
            send(
                gv.at[pl.ds(al(256 + e * 32, 32), 32)],
                cr.at[i],
                cs.at[i],
                (s, e * 2 + c),
            )
        )
    for i in range(1, 8):
        arrived(cr.at[i], cs.at[i])

    @pl.loop(0, 2)
    def _(r):
        here = pl.ds(al(r * 16, 16), 16)
        for q in range(4):
            cols = pl.ds(q * QUART, QUART)
            total = gv[pl.ds(al(256 + k * 32 + r * 16, 16), 16), cols].astype(F32)
            for i in range(1, 8):
                total += cr[i, here, cols].astype(F32)
            res[here, cols] = total.astype(BF16)

    stores.append(load(res, out_c, 17))
    for copy in stores:
        copy.wait()
    for copy in n_sends + r_sends + c_sends:
        copy.wait_send()

    @pl.when(s > 0)
    def _():
        for copy in p_sends:
            copy.wait_send()


def step(master, first, second, xo, xa, grads, wo, wa, ni):
    vm = pltpu.VMEM
    dma = pltpu.SemaphoreType.DMA
    anywhere = pl.BlockSpec(memory_space=pl.ANY)
    shape = jax.ShapeDtypeStruct
    flat = (ROWS, FEAT)
    new = pl.pallas_call(
        kernel,
        out_shape=(
            shape((OWN, FEAT), F32),
            shape((OWN, FEAT), F32),
            shape((OWN, FEAT), F32),
            shape((32, FEAT), BF16),
        ),
        in_specs=[anywhere] * 9,
        out_specs=[anywhere] * 4,
        scratch_shapes=[
            vm((FEAT, FEAT), BF16),
            vm(flat, BF16),
            vm((ROWS, HALF), BF16),
            vm((2, ROWS, FEAT), BF16),
            vm((2, ROWS, FEAT), BF16),
            vm((FEAT, HALF), F32),
            vm(flat, BF16),
            vm((TOK, FEAT), jnp.int32),
            vm((2, TOK, HALF), jnp.int32),
            vm((OWN, FEAT), F32),
            vm((4, ROWS, QUART), BF16),
            vm((2, 2, ROWS, QUART), BF16),
            vm((512, 256), BF16),
            vm((2, 2 * OWN, YW), BF16),
            vm((2, 2, 2 * OWN, YW), BF16),
            vm((2 * OWN, YW), BF16),
            vm((4, 2 * OWN, XW), BF16),
            vm((2, OWN, XW), BF16),
            vm((2, 2, OWN, XW), BF16),
            vm((OWN, HALF), F32),
            vm((256, FEAT), BF16),
            vm((8, 32, FEAT), BF16),
            vm((32, FEAT), BF16),
            dma((18,)),
            dma((96,)),
            dma((9,)),
            dma((10,)),
            dma((4,)),
            dma((16,)),
            dma((2, 2, 2)),
            dma((18,)),
            dma((4,)),
            dma((8,)),
        ],
        compiler_params=pltpu.CompilerParams(
            collective_id=0, has_side_effects=True, vmem_limit_bytes=67043328
        ),
        name="section_step",
    )(
        master[0],
        first[0],
        second[0],
        xo[0].reshape(flat),
        xa[0].reshape(flat),
        grads[0].reshape(flat),
        wo[0],
        wa[0],
        ni[0],
    )
    return tuple(value[None] for value in new)


def solution(mesh):
    row = P("section", "dp", None)
    deep = P("section", None, "dp", None)
    return jax.shard_map(
        step,
        mesh=mesh,
        in_specs=(row, row, row, deep, deep, deep, row, row, row),
        out_specs=(row, row, row, row),
        check_vma=False,
    )
```

```python
import jax
import jax.numpy as jnp
from jax import lax
from jax.experimental import pallas as pl
from jax.experimental.pallas import tpu as pltpu
from jax.sharding import PartitionSpec as P

LEAK_RATE = 0.5
LEARN_RATE = 0.002
FIRST_DECAY = 0.9
SECOND_DECAY = 0.95
EPSILON = 1e-08
WEIGHT_DECAY = 0.1
FIRST_CORRECTION = 1.0 - 0.9**10
SECOND_CORRECTION = 1.0 - 0.95**10

MESH = pl.DeviceIdType.MESH
F32, BF16 = jnp.float32, jnp.bfloat16
FEAT, HALF, QUART, OWN = 2560, 1280, 640, 160
ROWS, TOK, STEPS = 512, 128, 4
YW = 768
XW = HALF - YW


def al(value, by):
    return pl.multiple_of(value, by)


def kernel(
    master, first, second, xo, xa, grads, wo, wa, ni,
    out_p, out_m, out_v, out_c,
    wb, mo, mos, xov, xav, acc, gv, wov, wav, mst, outb, rcv, niw,
    r1, r23, rx, qx, q1, q23, gx, cz, cr, res,
    loc, snd, wr, ws, xs, nr, pr, rr, zr, cs,
):
    s, d = lax.axis_index("section"), lax.axis_index("dp")
    y, xh, c, k = d // 4, (d // 2) % 2, d % 2, d // 2
    yp, ym, y2 = (y + 1) % 4, (y + 3) % 4, (y + 2) % 4

    def index(y_, xh_, c_):
        return (y_ * 2 + xh_) * 2 + c_

    sib, xp = (s, index(y, xh, 1 - c)), (s, index(y, 1 - xh, c))
    up, down = (s, index(yp, xh, c)), (s, index(ym, xh, c))
    used = [0]

    def send(src, dst, sem, dev):
        copy = pltpu.make_async_remote_copy(
            src_ref=src, dst_ref=dst, send_sem=snd.at[used[0]], recv_sem=sem,
            device_id=dev, device_id_type=MESH,
        )
        used[0] += 1
        copy.start()
        return copy

    def arrived(dst, sem):
        pltpu.make_async_remote_copy(
            src_ref=dst, dst_ref=dst, send_sem=snd.at[0], recv_sem=sem,
            device_id=sib, device_id_type=MESH,
        ).wait_recv()

    def load(src, dst, i):
        copy = pltpu.make_async_copy(src, dst, loc.at[i])
        copy.start()
        return copy

    def owner(y_, xh_, c_, part=0, rows=OWN):
        return wb.at[pl.ds(al(index(y_, xh_, c_) * OWN + part, 16), rows)]

    def half(which):
        return pl.ds(al(which * HALF, 128), HALF)

    l_mst = load(master, mst, 0)
    l_g = load(grads, gv, 1)
    l_wo = load(wo, wov, 2)
    l_xo = load(xo, xov.at[c], 3)
    l_xa = load(xa, xav.at[c], 4)
    l_wa = load(wa.at[:, half(c)], wav.at[c], 5)

    def base(e):
        return al(e * OWN - (e % 4) * 32, 128)

    l_ni = load(
        ni.at[:, pl.ds(base(d), 256)], niw.at[pl.ds(al(c * 256 + k * 32, 32), 32)], 6
    )

    barrier = pltpu.get_barrier_semaphore()
    for i in range(1, 16):
        pl.semaphore_signal(barrier, inc=1, device_id=(s, (d + i) % 16), device_id_type=MESH)

    @pl.when(s > 0)
    def _():
        for h in range(2):
            pl.semaphore_signal(barrier, inc=1, device_id=(s - 1, k * 2 + h), device_id_type=MESH)

    @pl.when(s < 7)
    def _():
        for h in range(2):
            pl.semaphore_signal(barrier, inc=1, device_id=(s + 1, k * 2 + h), device_id_type=MESH)

    l_mst.wait()

    @pl.loop(0, OWN // 16)
    def _(r):
        wb[pl.ds(al(d * OWN + r * 16, 16), 16), :] = mst[pl.ds(al(r * 16, 16), 16), :].astype(BF16)

    pl.semaphore_wait(barrier, 15 + 2 * jnp.minimum(s, 1) + 2 * jnp.minimum(7 - s, 1))

    mine = owner(y, xh, c)
    w_sends = [
        send(mine, mine, wr.at[0], xp),
        send(mine, mine, wr.at[1], up),
        send(mine, mine, wr.at[2], down),
        send(mine, mine, ws.at[0], sib),
    ]
    x_sends = [
        send(xo, xov.at[c], xs.at[0], sib),
        send(wa.at[:, half(1 - c)], wav.at[c], xs.at[1], sib),
    ]
    l_g.wait()
    l_wo.wait()

    @pl.loop(0, TOK // 16)
    def _(r):
        for q in range(4):
            cols = pl.ds(q * QUART, QUART)
            bits = wov[pl.ds(al(r * 16, 16), 16), cols]
            carry = jnp.zeros((16, QUART), F32)
            for t in reversed(range(STEPS)):
                rows = pl.ds(al(t * TOK + r * 16, 16), 16)
                window = ((bits >> t) & 1).astype(F32)
                carry = window * gv[rows, cols].astype(F32) + LEAK_RATE * carry
                mo[rows, cols] = carry.astype(BF16)

    x_sends.append(send(mo.at[:, half(1 - c)], mos, xs.at[3], sib))
    x_sends.append(send(xa, xav.at[c], xs.at[2], sib))

    p_sends = []

    parts = ((xh * 384, 256), ((1 - xh) * 256, 384))

    def outgoing(b, n, part):
        begin, width = parts[part]
        cols = pl.ds(al(begin, 128), width)
        wide = pl.ds(al(b * QUART + begin, 128), width)
        for h in (1, 0):
            rows = pl.ds(h * 256, 256)
            through = lax.dot_general(
                mo[rows, :], wb[wide, :], (((1,), (1,)), ((), ())), preferred_element_type=F32
            )
            outb[n, rows, cols] = (gv[rows, wide].astype(F32) + through).astype(BF16)
            copy = pltpu.make_async_remote_copy(
                src_ref=outb.at[n, rows, cols],
                dst_ref=rcv.at[c, b % 2, rows, cols],
                send_sem=snd.at[used[0]],
                recv_sem=pr.at[c, b % 2, part, h],
                device_id=(s - 1, k * 2 + b // 2),
                device_id_type=MESH,
            )
            used[0] += 1
            p_sends.append(copy)
            pl.when(s > 0)(copy.start)

    def relay(kind, piece, *targets):
        arrived(piece, wr.at[kind])
        for region, sem, dev in targets:
            w_sends.append(send(region, region, sem, dev))

    arrived(owner(y, xh, 1 - c), ws.at[0])
    outgoing(y, 0, 0)
    piece = owner(y, 1 - xh, c)
    relay(0, piece, (piece, wr.at[3], up), (piece, wr.at[4], down), (piece, ws.at[1], sib))
    piece = owner(ym, xh, c)
    relay(1, piece, (owner(ym, xh, c, 0, 80), wr.at[5], up), (piece, ws.at[2], sib))
    piece = owner(yp, xh, c)
    relay(2, piece, (owner(yp, xh, c, 80, 80), wr.at[6], down), (piece, ws.at[3], sib))
    arrived(owner(y, 1 - xh, 1 - c), ws.at[1])
    outgoing(y, 0, 1)
    arrived(owner(ym, xh, 1 - c), ws.at[2])
    outgoing(ym, 1, 0)
    arrived(owner(yp, xh, 1 - c), ws.at[3])
    outgoing(yp, 2, 0)

    across = (((0,), (0,)), ((), ()))
    l_xo.wait()
    arrived(xov.at[1 - c], xs.at[0])
    arrived(mos, xs.at[3])

    @pl.loop(0, 4)
    def _(b):
        rows = pl.ds(al(b * QUART, 128), QUART)
        for j in range(2):
            acc[rows, pl.ds(j * QUART, QUART)] = lax.dot_general(
                xov[c, :, rows],
                mo[:, pl.ds(al(c * HALF + j * QUART, 128), QUART)],
                across,
                preferred_element_type=F32,
            ) + lax.dot_general(
                xov[1 - c, :, rows],
                mos[:, pl.ds(j * QUART, QUART)],
                across,
                preferred_element_type=F32,
            )

    piece = owner(ym, 1 - xh, c)
    relay(3, piece, (owner(ym, 1 - xh, c, 0, 80), wr.at[7], up), (piece, ws.at[4], sib))
    piece = owner(yp, 1 - xh, c)
    relay(4, piece, (owner(yp, 1 - xh, c, 80, 80), wr.at[8], down), (piece, ws.at[5], sib))
    arrived(owner(ym, 1 - xh, 1 - c), ws.at[4])
    outgoing(ym, 1, 1)
    arrived(owner(yp, 1 - xh, 1 - c), ws.at[5])
    outgoing(yp, 2, 1)
    for n, xh_ in enumerate((xh, 1 - xh)):
        for i in range(2):
            piece = owner(y2, xh_, c, 80 * i, 80)
            relay(5 + 2 * n + i, piece, (piece, ws.at[6 + 2 * n + i], sib))
        for i in range(2):
            arrived(owner(y2, xh_, 1 - c, 80 * i, 80), ws.at[6 + 2 * n + i])
        outgoing(y2, 3, n)

    def far(b):
        away = (b - y + 4) % 4
        return jnp.minimum(away, 4 - away)

    early = jnp.where(far(2 * c) < far(2 * c + 1), 0, 1)
    late = 1 - early
    l_xa.wait()
    arrived(xav.at[1 - c], xs.at[2])
    l_wa.wait()
    arrived(wav.at[1 - c], xs.at[1])

    def arriving(j):
        for cc in range(2):
            for part, (begin, width) in enumerate(parts):
                for h in (1, 0):
                    arrived(
                        rcv.at[cc, j, pl.ds(h * 256, 256), pl.ds(al(begin, 128), width)],
                        pr.at[cc, j, part, h],
                    )

            @pl.loop(0, TOK // 16)
            def _(r, cc=cc):
                bits = wav[cc, pl.ds(al(r * 16, 16), 16), pl.ds(al(j * QUART, 128), QUART)]
                carry = jnp.zeros((16, QUART), F32)
                for t in reversed(range(STEPS)):
                    rows = pl.ds(al(t * TOK + r * 16, 16), 16)
                    window = ((bits >> t) & 1).astype(F32)
                    carry = window * rcv[cc, j, rows, :].astype(F32) + LEAK_RATE * carry
                    rcv[cc, j, rows, :] = carry.astype(BF16)

    def more(b, j):
        rows = pl.ds(al(b * QUART, 128), QUART)
        cols = pl.ds(al(j * QUART, 128), QUART)
        acc[rows, cols] += lax.dot_general(
            xav[0, :, rows], rcv[0, j], across, preferred_element_type=F32
        ) + lax.dot_general(xav[1, :, rows], rcv[1, j], across, preferred_element_type=F32)

    @pl.when(s < 7)
    def _():
        arriving(early)

        @pl.loop(0, 4)
        def _(b):
            more(b, early)

        arriving(late)

    for copy in w_sends + x_sends:
        copy.wait_send()

    def unit(y_, xh_, n=2, first_=0):
        return pl.ds(al((y_ * 2 + xh_) * 2 * OWN + first_ * OWN, 32), n * OWN)

    def rounded(b):
        @pl.loop(0, QUART // 32)
        def _(r):
            rows = pl.ds(al(b * QUART + r * 32, 32), 32)
            wb[rows, pl.ds(0, HALF)] = acc[rows, :].astype(BF16)

    def finish(b):
        @pl.when(s < 7)
        def _():
            more(b, late)

        rounded(b)

    ycol, xcol = pl.ds(0, YW), pl.ds(YW, XW)
    r_sends = []

    def to_partner(b, n):
        r_sends.append(send(wb.at[unit(b, 1 - xh), xcol], qx.at[n], rr.at[7 + n], xp))

    finish(y2)
    r_sends.append(send(wb.at[unit(y2, 0), ycol], r1.at[0], rr.at[0], up))
    r_sends.append(send(wb.at[unit(y2, 1), ycol], r1.at[1], rr.at[1], down))
    to_partner(y2, 0)
    finish(yp)
    r_sends.append(send(wb.at[unit(yp, 1), ycol], r23.at[0, 1], rr.at[3], up))
    to_partner(yp, 1)
    finish(ym)
    r_sends.append(send(wb.at[unit(ym, 0), ycol], r23.at[1, 0], rr.at[4], down))
    to_partner(ym, 2)
    finish(y)
    to_partner(y, 3)
    n_sends = []
    for i in range(1, 16):
        e = (d + i) % 16
        n_sends.append(
            send(
                ni.at[:, pl.ds(base(e), 256)],
                niw.at[pl.ds(al(c * 256 + k * 32, 32), 32)],
                nr.at[i],
                (s, e),
            )
        )


    def add(start, count, cols, *terms, to=None, keep=False):
        @pl.loop(0, count // 32)
        def _(r):
            rows = pl.ds(al(start + r * 32, 32), 32)
            total = acc[rows, cols]
            for term in terms:
                total += term[pl.ds(al(r * 32, 32), 32), :].astype(F32)
            if keep:
                acc[rows, cols] = total
            else:
                wb[rows, cols] = total.astype(BF16)

    def at_unit(y_, xh_, c_=0):
        return index(y_, xh_, c_) * OWN

    arrived(r1.at[0], rr.at[0])
    add(at_unit(yp, 0), 2 * OWN, ycol, r1.at[0])
    r_sends.append(send(wb.at[unit(yp, 0), ycol], r23.at[0, 0], rr.at[2], up))
    arrived(r1.at[1], rr.at[1])
    add(at_unit(ym, 1), 2 * OWN, ycol, r1.at[1])
    r_sends.append(send(wb.at[unit(ym, 1), ycol], r23.at[1, 1], rr.at[5], down))

    arrived(qx.at[0], rr.at[7])
    add(at_unit(y2, xh), 2 * OWN, xcol, qx.at[0])
    r_sends.append(send(wb.at[unit(y2, xh, 1, 0), xcol], q1.at[0], rr.at[11], up))
    r_sends.append(send(wb.at[unit(y2, xh, 1, 1), xcol], q1.at[1], rr.at[12], down))
    arrived(qx.at[1], rr.at[8])
    add(at_unit(yp, xh, 1), OWN, xcol, qx.at[1, pl.ds(OWN, OWN)])
    r_sends.append(send(wb.at[unit(yp, xh, 1, 1), xcol], q23.at[0, 1], rr.at[14], up))
    add(at_unit(yp, xh, 0), OWN, xcol, qx.at[1, pl.ds(0, OWN)], keep=True)
    arrived(qx.at[2], rr.at[9])
    add(at_unit(ym, xh, 0), OWN, xcol, qx.at[2, pl.ds(0, OWN)])
    r_sends.append(send(wb.at[unit(ym, xh, 1, 0), xcol], q23.at[1, 0], rr.at[15], down))
    add(at_unit(ym, xh, 1), OWN, xcol, qx.at[2, pl.ds(OWN, OWN)], keep=True)
    l_m = [load(first.at[:, half(h)], acc.at[unit(y2, h, 1, 0)], 7 + h) for h in range(2)]
    l_v = [load(second.at[:, half(h)], acc.at[unit(y2, h, 1, 1)], 9 + h) for h in range(2)]

    arrived(r23.at[0, 1], rr.at[3])
    arrived(r23.at[1, 0], rr.at[4])
    arrived(r23.at[0, 0], rr.at[2])
    arrived(r23.at[1, 1], rr.at[5])
    arrived(qx.at[3], rr.at[10])
    add(at_unit(y, 1 - xh), 2 * OWN, ycol, r23.at[0, 1 - xh], r23.at[1, 1 - xh])
    r_sends.append(send(wb.at[unit(y, 1 - xh), ycol], rx, rr.at[6], xp))
    add(at_unit(y, xh), 2 * OWN, ycol, r23.at[0, xh], r23.at[1, xh], keep=True)

    arrived(q1.at[0], rr.at[11])
    add(at_unit(yp, xh, 0), OWN, xcol, q1.at[0])
    r_sends.append(send(wb.at[unit(yp, xh, 1, 0), xcol], q23.at[0, 0], rr.at[13], up))
    arrived(q1.at[1], rr.at[12])
    add(at_unit(ym, xh, 1), OWN, xcol, q1.at[1])
    r_sends.append(send(wb.at[unit(ym, xh, 1, 1), xcol], q23.at[1, 1], rr.at[16], down))
    for u in range(2):
        arrived(q23.at[0, 1 - u], rr.at[13 + (1 - u)])
        arrived(q23.at[1, u], rr.at[15 + u])
    for u in range(2):
        add(
            at_unit(y, xh, u), OWN, xcol,
            qx.at[3, pl.ds(u * OWN, OWN)], q23.at[0, u], q23.at[1, u], keep=True,
        )
    arrived(rx, rr.at[6])
    add(at_unit(y, xh), 2 * OWN, ycol, rx, keep=True)

    r_sends.append(send(acc.at[pl.ds(al(at_unit(y, xh, 1 - c), 32), OWN)], gx, rr.at[17], sib))

    @pl.loop(0, 256 // 32)
    def _(r):
        mo[pl.ds(al(r * 32, 32), 32), :] = jnp.zeros((32, FEAT), BF16)

    for copy in l_m + l_v:
        copy.wait()
    shift = (d % 4) * 32
    stores = []

    def adam(which, gradient, start):
        @pl.loop(0, OWN // 16)
        def _(r):
            here = pl.ds(al(r * 16, 16), 16)
            cols = half(which)
            at_m = pl.ds(al(at_unit(y2, which, 0) + r * 16, 16), 16)
            at_v = pl.ds(al(at_unit(y2, which, 1) + r * 16, 16), 16)
            g = gradient[pl.ds(al(start + r * 16, 16), 16), :]
            params = mst[here, cols]
            m = FIRST_DECAY * acc[at_m, :] + (1.0 - FIRST_DECAY) * g
            v = SECOND_DECAY * acc[at_v, :] + (1.0 - SECOND_DECAY) * g * g
            acc[at_m, :] = m
            acc[at_v, :] = v
            direction = m / FIRST_CORRECTION / (jnp.sqrt(v / SECOND_CORRECTION) + EPSILON)
            new = params - LEARN_RATE * (direction + WEIGHT_DECAY * params)
            mst[here, cols] = new
            mo[pl.ds(al(shift + r * 16, 16), 16), cols] = new.astype(BF16)

        n = 11 if which is c else 14
        stores.append(load(mst.at[:, half(which)], out_p.at[:, half(which)], n))
        stores.append(load(acc.at[unit(y2, which, 1, 0)], out_m.at[:, half(which)], n + 1))
        stores.append(load(acc.at[unit(y2, which, 1, 1)], out_v.at[:, half(which)], n + 2))

    adam(c, acc, at_unit(y, xh, c))
    arrived(gx, rr.at[17])
    adam(1 - c, gx, 0)

    l_ni.wait()
    for i in range(1, 16):
        e = (d - i + 16) % 16
        arrived(niw.at[pl.ds(al((e % 2) * 256 + (e // 2) * 32, 32), 32)], nr.at[i])
    c_sends = []
    for q in range(4):
        cols = pl.ds(q * QUART, QUART)
        gv[pl.ds(0, 256), cols] = jnp.dot(
            niw[pl.ds(al((1 - c) * 256, 256), 256), :],
            mo[pl.ds(0, 256), cols],
            preferred_element_type=F32,
        ).astype(BF16)
        c_sends.append(send(gv.at[pl.ds(0, 256), cols], cz.at[:, cols], zr.at[q], sib))
    for q in range(4):
        cols = pl.ds(q * QUART, QUART)
        total = jnp.dot(
            niw[pl.ds(al(c * 256, 256), 256), :],
            mo[pl.ds(0, 256), cols],
            preferred_element_type=F32,
        )
        arrived(cz.at[:, cols], zr.at[q])
        gv[pl.ds(256, 256), cols] = (total + cz[:, cols].astype(F32)).astype(BF16)
    for i in range(1, 8):
        e = (k + i) % 8
        c_sends.append(
            send(
                gv.at[pl.ds(al(256 + e * 32, 32), 32)],
                cr.at[i],
                cs.at[i],
                (s, e * 2 + c),
            )
        )
    for i in range(1, 8):
        arrived(cr.at[i], cs.at[i])

    @pl.loop(0, 2)
    def _(r):
        here = pl.ds(al(r * 16, 16), 16)
        for q in range(4):
            cols = pl.ds(q * QUART, QUART)
            total = gv[pl.ds(al(256 + k * 32 + r * 16, 16), 16), cols].astype(F32)
            for i in range(1, 8):
                total += cr[i, here, cols].astype(F32)
            res[here, cols] = total.astype(BF16)

    stores.append(load(res, out_c, 17))
    for copy in stores:
        copy.wait()
    for copy in n_sends + r_sends + c_sends:
        copy.wait_send()

    @pl.when(s > 0)
    def _():
        for copy in p_sends:
            copy.wait_send()


def settle_kernel(*refs):
    count = len(refs) // 4
    sources, targets, held, sems = (refs[i * count : (i + 1) * count] for i in range(4))
    taken = [pltpu.make_async_copy(a, v, m.at[0]) for a, v, m in zip(sources, held, sems)]
    given = [pltpu.make_async_copy(v, b, m.at[1]) for v, b, m in zip(held, targets, sems)]
    for copy in taken:
        copy.start()
    for copy, onward in zip(taken, given):
        copy.wait()
        onward.start()
    for copy in given:
        copy.wait()


def settle(*values):
    anywhere = pl.BlockSpec(memory_space=pl.ANY)
    return pl.pallas_call(
        settle_kernel,
        out_shape=tuple(jax.ShapeDtypeStruct(v.shape, v.dtype) for v in values),
        in_specs=[anywhere] * len(values),
        out_specs=[anywhere] * len(values),
        scratch_shapes=[pltpu.VMEM(v.shape, v.dtype) for v in values]
        + [pltpu.SemaphoreType.DMA((2,)) for _ in values],
        name="settle",
    )(*values)


def step(master, first, second, xo, xa, grads, wo, wa, ni):
    vm = pltpu.VMEM
    dma = pltpu.SemaphoreType.DMA
    anywhere = pl.BlockSpec(memory_space=pl.ANY)
    shape = jax.ShapeDtypeStruct
    flat = (ROWS, FEAT)
    new = pl.pallas_call(
        kernel,
        out_shape=(
            shape((OWN, FEAT), F32),
            shape((OWN, FEAT), F32),
            shape((OWN, FEAT), F32),
            shape((32, FEAT), BF16),
        ),
        in_specs=[anywhere] * 9,
        out_specs=[anywhere] * 4,
        scratch_shapes=[
            vm((FEAT, FEAT), BF16),
            vm(flat, BF16),
            vm((ROWS, HALF), BF16),
            vm((2, ROWS, FEAT), BF16),
            vm((2, ROWS, FEAT), BF16),
            vm((FEAT, HALF), F32),
            vm(flat, BF16),
            vm((TOK, FEAT), jnp.int32),
            vm((2, TOK, HALF), jnp.int32),
            vm((OWN, FEAT), F32),
            vm((4, ROWS, QUART), BF16),
            vm((2, 2, ROWS, QUART), BF16),
            vm((512, 256), BF16),
            vm((2, 2 * OWN, YW), BF16),
            vm((2, 2, 2 * OWN, YW), BF16),
            vm((2 * OWN, YW), BF16),
            vm((4, 2 * OWN, XW), BF16),
            vm((2, OWN, XW), BF16),
            vm((2, 2, OWN, XW), BF16),
            vm((OWN, HALF), F32),
            vm((256, FEAT), BF16),
            vm((8, 32, FEAT), BF16),
            vm((32, FEAT), BF16),
            dma((18,)),
            dma((112,)),
            dma((9,)),
            dma((10,)),
            dma((4,)),
            dma((16,)),
            dma((2, 2, 2, 2)),
            dma((18,)),
            dma((4,)),
            dma((8,)),
        ],
        compiler_params=pltpu.CompilerParams(
            collective_id=0, has_side_effects=True, vmem_limit_bytes=67043328
        ),
        name="section_step",
    )(
        master[0],
        first[0],
        second[0],
        xo[0].reshape(flat),
        xa[0].reshape(flat),
        grads[0].reshape(flat),
        wo[0],
        wa[0],
        ni[0],
    )
    return tuple(value[None] for value in settle(*new))


def solution(mesh):
    row = P("section", "dp", None)
    deep = P("section", None, "dp", None)
    return jax.shard_map(
        step,
        mesh=mesh,
        in_specs=(row, row, row, deep, deep, deep, row, row, row),
        out_specs=(row, row, row, row),
        check_vma=False,
    )
```

```python
import jax
import jax.numpy as jnp
from jax import lax
from jax.experimental import pallas as pl
from jax.experimental.pallas import tpu as pltpu
from jax.sharding import PartitionSpec as P

LEAK_RATE = 0.5
LEARN_RATE = 0.002
FIRST_DECAY = 0.9
SECOND_DECAY = 0.95
EPSILON = 1e-08
WEIGHT_DECAY = 0.1
FIRST_CORRECTION = 1.0 - 0.9**10
SECOND_CORRECTION = 1.0 - 0.95**10

MESH = pl.DeviceIdType.MESH
F32, BF16 = jnp.float32, jnp.bfloat16
FEAT, HALF, QUART, OWN = 2560, 1280, 640, 160
ROWS, TOK, STEPS = 512, 128, 4
PART, MID = 256, 128
PAIR, MIDS = 2 * PART, 2 * MID


def al(value, by):
    return pl.multiple_of(value, by)


def kernel(
    master, first, second, xo, xa, grads, wo, wa, ni,
    out_p, out_m, out_v, out_c,
    wb, mo, mos, xov, xav, acc, gv, wov, wav, mst, outb, rcv, niw,
    n1, n23, r1, r23, rx, qx, q1, q23, gx, cz, cr, res,
    loc, snd, wr, ws, xs, nr, pr, rr, zr, cs,
):
    s, d = lax.axis_index("section"), lax.axis_index("dp")
    y, xh, c, k = d // 4, (d // 2) % 2, d % 2, d // 2
    yp, ym, y2 = (y + 1) % 4, (y + 3) % 4, (y + 2) % 4

    def index(y_, xh_, c_):
        return (y_ * 2 + xh_) * 2 + c_

    sib, xp = (s, index(y, xh, 1 - c)), (s, index(y, 1 - xh, c))
    up, down = (s, index(yp, xh, c)), (s, index(ym, xh, c))
    used = [0]

    def send(src, dst, sem, dev):
        copy = pltpu.make_async_remote_copy(
            src_ref=src, dst_ref=dst, send_sem=snd.at[used[0]], recv_sem=sem,
            device_id=dev, device_id_type=MESH,
        )
        used[0] += 1
        copy.start()
        return copy

    def arrived(dst, sem):
        pltpu.make_async_remote_copy(
            src_ref=dst, dst_ref=dst, send_sem=snd.at[0], recv_sem=sem,
            device_id=sib, device_id_type=MESH,
        ).wait_recv()

    def load(src, dst, i):
        copy = pltpu.make_async_copy(src, dst, loc.at[i])
        copy.start()
        return copy

    def owner(y_, xh_, c_, part=0, rows=OWN):
        return wb.at[pl.ds(al(index(y_, xh_, c_) * OWN + part, 16), rows)]

    def half(which):
        return pl.ds(al(which * HALF, 128), HALF)

    l_mst = load(master, mst, 0)
    l_g = load(grads, gv, 1)
    l_wo = load(wo, wov, 2)
    l_xo = load(xo, xov.at[c], 3)
    l_xa = load(xa, xav.at[c], 4)
    l_wa = load(wa.at[:, half(c)], wav.at[c], 5)

    def base(e):
        return al(e * OWN - (e % 4) * 32, 128)

    l_ni = load(
        ni.at[:, pl.ds(base(d), 256)], niw.at[pl.ds(al(c * 256 + k * 32, 32), 32)], 6
    )

    barrier = pltpu.get_barrier_semaphore()
    for i in range(1, 16):
        pl.semaphore_signal(barrier, inc=1, device_id=(s, (d + i) % 16), device_id_type=MESH)

    @pl.when(s > 0)
    def _():
        for h in range(2):
            pl.semaphore_signal(barrier, inc=1, device_id=(s - 1, k * 2 + h), device_id_type=MESH)

    @pl.when(s < 7)
    def _():
        for h in range(2):
            pl.semaphore_signal(barrier, inc=1, device_id=(s + 1, k * 2 + h), device_id_type=MESH)

    l_mst.wait()

    @pl.loop(0, OWN // 16)
    def _(r):
        wb[pl.ds(al(d * OWN + r * 16, 16), 16), :] = mst[pl.ds(al(r * 16, 16), 16), :].astype(BF16)

    pl.semaphore_wait(barrier, 15 + 2 * jnp.minimum(s, 1) + 2 * jnp.minimum(7 - s, 1))

    mine = owner(y, xh, c)
    w_sends = [
        send(mine, mine, wr.at[0], xp),
        send(mine, mine, wr.at[1], up),
        send(mine, mine, wr.at[2], down),
        send(mine, mine, ws.at[0], sib),
    ]
    x_sends = [
        send(xo, xov.at[c], xs.at[0], sib),
        send(wa.at[:, half(1 - c)], wav.at[c], xs.at[1], sib),
    ]
    l_g.wait()
    l_wo.wait()

    @pl.loop(0, TOK // 16)
    def _(r):
        for q in range(4):
            cols = pl.ds(q * QUART, QUART)
            bits = wov[pl.ds(al(r * 16, 16), 16), cols]
            carry = jnp.zeros((16, QUART), F32)
            for t in reversed(range(STEPS)):
                rows = pl.ds(al(t * TOK + r * 16, 16), 16)
                window = ((bits >> t) & 1).astype(F32)
                carry = window * gv[rows, cols].astype(F32) + LEAK_RATE * carry
                mo[rows, cols] = carry.astype(BF16)

    x_sends.append(send(mo.at[:, half(1 - c)], mos, xs.at[3], sib))
    x_sends.append(send(xa, xav.at[c], xs.at[2], sib))

    p_sends = []

    parts = ((xh * 384, 256), ((1 - xh) * 256, 384))

    def outgoing(b, n, part):
        begin, width = parts[part]
        cols = pl.ds(al(begin, 128), width)
        wide = pl.ds(al(b * QUART + begin, 128), width)
        for h in (1, 0):
            rows = pl.ds(h * 256, 256)
            through = lax.dot_general(
                mo[rows, :], wb[wide, :], (((1,), (1,)), ((), ())), preferred_element_type=F32
            )
            outb[n, rows, cols] = (gv[rows, wide].astype(F32) + through).astype(BF16)
            copy = pltpu.make_async_remote_copy(
                src_ref=outb.at[n, rows, cols],
                dst_ref=rcv.at[c, b % 2, rows, cols],
                send_sem=snd.at[used[0]],
                recv_sem=pr.at[c, b % 2, part, h],
                device_id=(s - 1, k * 2 + b // 2),
                device_id_type=MESH,
            )
            used[0] += 1
            p_sends.append(copy)
            pl.when(s > 0)(copy.start)

    def relay(kind, piece, *targets):
        arrived(piece, wr.at[kind])
        for region, sem, dev in targets:
            w_sends.append(send(region, region, sem, dev))

    arrived(owner(y, xh, 1 - c), ws.at[0])
    outgoing(y, 0, 0)
    piece = owner(ym, xh, c)
    relay(1, piece, (owner(ym, xh, c, 0, 80), wr.at[5], up), (piece, ws.at[2], sib))
    piece = owner(yp, xh, c)
    relay(2, piece, (owner(yp, xh, c, 80, 80), wr.at[6], down), (piece, ws.at[3], sib))
    piece = owner(y, 1 - xh, c)
    relay(0, piece, (piece, wr.at[3], up), (piece, wr.at[4], down), (piece, ws.at[1], sib))
    arrived(owner(y, 1 - xh, 1 - c), ws.at[1])
    outgoing(y, 0, 1)
    arrived(owner(ym, xh, 1 - c), ws.at[2])
    outgoing(ym, 1, 0)
    arrived(owner(yp, xh, 1 - c), ws.at[3])
    outgoing(yp, 2, 0)

    across = (((0,), (0,)), ((), ()))
    l_xo.wait()
    arrived(xov.at[1 - c], xs.at[0])
    arrived(mos, xs.at[3])

    @pl.loop(0, 4)
    def _(b):
        rows = pl.ds(al(b * QUART, 128), QUART)
        for j in range(2):
            acc[rows, pl.ds(j * QUART, QUART)] = lax.dot_general(
                xov[c, :, rows],
                mo[:, pl.ds(al(c * HALF + j * QUART, 128), QUART)],
                across,
                preferred_element_type=F32,
            ) + lax.dot_general(
                xov[1 - c, :, rows],
                mos[:, pl.ds(j * QUART, QUART)],
                across,
                preferred_element_type=F32,
            )

    def far_block(xh_, n):
        for i in range(2):
            piece = owner(y2, xh_, c, 80 * i, 80)
            relay(5 + 2 * n + i, piece, (piece, ws.at[6 + 2 * n + i], sib))
        for i in range(2):
            arrived(owner(y2, xh_, 1 - c, 80 * i, 80), ws.at[6 + 2 * n + i])
        outgoing(y2, 3, n)

    far_block(xh, 0)
    piece = owner(ym, 1 - xh, c)
    relay(3, piece, (owner(ym, 1 - xh, c, 0, 80), wr.at[7], up), (piece, ws.at[4], sib))
    piece = owner(yp, 1 - xh, c)
    relay(4, piece, (owner(yp, 1 - xh, c, 80, 80), wr.at[8], down), (piece, ws.at[5], sib))
    arrived(owner(ym, 1 - xh, 1 - c), ws.at[4])
    outgoing(ym, 1, 1)
    arrived(owner(yp, 1 - xh, 1 - c), ws.at[5])
    outgoing(yp, 2, 1)

    l_xa.wait()
    arrived(xav.at[1 - c], xs.at[2])
    l_wa.wait()
    arrived(wav.at[1 - c], xs.at[1])

    def arriving(part):
        begin, width = parts[part]
        cols = pl.ds(al(begin, 128), width)
        for j in range(2):
            for cc in range(2):
                for h in (1, 0):
                    arrived(rcv.at[cc, j, pl.ds(h * 256, 256), cols], pr.at[cc, j, part, h])

                @pl.loop(0, TOK // 16)
                def _(r, cc=cc, j=j):
                    here = pl.ds(al(r * 16, 16), 16)
                    bits = wav[cc, here, pl.ds(al(j * QUART + begin, 128), width)]
                    carry = jnp.zeros((16, width), F32)
                    for t in reversed(range(STEPS)):
                        rows = pl.ds(al(t * TOK + r * 16, 16), 16)
                        window = ((bits >> t) & 1).astype(F32)
                        carry = window * rcv[cc, j, rows, cols].astype(F32) + LEAK_RATE * carry
                        rcv[cc, j, rows, cols] = carry.astype(BF16)

    def more(b, part):
        begin, width = parts[part]
        rows = pl.ds(al(b * QUART, 128), QUART)
        cols = pl.ds(al(begin, 128), width)

        @pl.when(s < 7)
        def _():
            for j in range(2):
                acc[rows, pl.ds(al(j * QUART + begin, 128), width)] += lax.dot_general(
                    xav[0, :, rows], rcv[0, j, :, cols], across, preferred_element_type=F32
                ) + lax.dot_general(
                    xav[1, :, rows], rcv[1, j, :, cols], across, preferred_element_type=F32
                )

    near, rest, mid = (xh * 384, PART), ((1 - xh) * 384, PART), (PART, MID)
    r_sends = []

    def at_unit(y_, xh_, c_=0):
        return index(y_, xh_, c_) * OWN

    def unit(y_, xh_, n=2, first_=0):
        return pl.ds(al(at_unit(y_, xh_, first_), 32), n * OWN)

    def add(start, count, group, *terms, to=None):
        begin, width = group
        height = 32

        @pl.loop(0, count // height)
        def _(r):
            rows = pl.ds(al(start + r * height, 32), height)
            here = pl.ds(al(r * height, 32), height)
            for j in range(2):
                cols = pl.ds(al(j * QUART + begin, 128), width)
                side = pl.ds(j * width, width)
                total = acc[rows, cols]
                for term in terms:
                    total += term[here, side].astype(F32)
                if to is None:
                    acc[rows, cols] = total
                else:
                    to[here, side] = total.astype(BF16)

    def pass_on(src, dst, sem, dev):
        r_sends.append(send(src, dst, sem, dev))

    class AlongY:
        def __init__(self, group, place, one, two, sems):
            self.group, self.place, self.one, self.two, self.sems = group, place, one, two, sems

        def begin(self, b):
            for xh_ in range(2):
                keep = (b is yp and xh_ == 0) or (b is ym and xh_ == 1) or b is y
                if keep:
                    continue
                ref = self.place(b, xh_)
                add(at_unit(b, xh_), 2 * OWN, self.group, to=ref)
                if b is y2:
                    pass_on(ref, self.one.at[xh_], rr.at[self.sems + xh_], (up, down)[xh_])
                elif b is yp:
                    pass_on(ref, self.two.at[0, 1], rr.at[self.sems + 3], up)
                else:
                    pass_on(ref, self.two.at[1, 0], rr.at[self.sems + 4], down)

        def middle(self):
            for xh_, b, dev, sem in ((0, yp, up, 2), (1, ym, down, 5)):
                arrived(self.one.at[xh_], rr.at[self.sems + xh_])
                ref = self.place(b, xh_)
                add(at_unit(b, xh_), 2 * OWN, self.group, self.one.at[xh_], to=ref)
                pass_on(ref, self.two.at[xh_, xh_], rr.at[self.sems + sem], dev)

        def end(self, there, sem):
            for i, h, sem_ in ((0, 1, 3), (1, 0, 4), (0, 0, 2), (1, 1, 5)):
                arrived(self.two.at[i, h], rr.at[self.sems + sem_])
            other = self.place(y, 1 - xh)
            add(
                at_unit(y, 1 - xh), 2 * OWN, self.group,
                self.two.at[0, 1 - xh], self.two.at[1, 1 - xh], to=other,
            )
            pass_on(other, there, sem, xp)
            add(at_unit(y, xh), 2 * OWN, self.group, self.two.at[0, xh], self.two.at[1, xh])

    def near_place(b, xh_):
        chip = b * 2 + xh_
        return xov.at[chip // 5, pl.ds(0, 2 * OWN), pl.ds(al((chip % 5) * PAIR, 128), PAIR)]

    def rest_place(b, xh_):
        return wb.at[unit(b, xh_), pl.ds(0, PAIR)]

    along_near = AlongY(near, near_place, n1, n23, 0)
    along_rest = AlongY(rest, rest_place, r1, r23, 6)

    pl.when(s < 7)(lambda: arriving(0))
    for b in (y2, yp, ym, y):
        more(b, 0)
        along_near.begin(b)

    far_block(1 - xh, 1)
    along_near.middle()
    for copy in w_sends + x_sends:
        copy.wait_send()
    pl.when(s < 7)(lambda: arriving(1))
    mcol = pl.ds(PAIR, MIDS)

    for n, b in enumerate((y2, yp, ym, y)):
        more(b, 1)
        along_rest.begin(b)
        ref = wb.at[unit(b, 1 - xh), mcol]
        add(at_unit(b, 1 - xh), 2 * OWN, mid, to=ref)
        pass_on(ref, qx.at[n], rr.at[14 + n], xp)
    n_sends = []
    for i in range(1, 16):
        e = (d + i) % 16
        n_sends.append(
            send(
                ni.at[:, pl.ds(base(e), 256)],
                niw.at[pl.ds(al(c * 256 + k * 32, 32), 32)],
                nr.at[i],
                (s, e),
            )
        )


    along_rest.middle()
    along_near.end(rx.at[0], rr.at[12])

    def one_unit(y_, u):
        return wb.at[unit(y_, xh, 1, u), mcol]

    def mid_sum(y_, u, n):
        return at_unit(y_, xh, u), OWN, mid, qx.at[n, pl.ds(u * OWN, OWN)]

    arrived(qx.at[0], rr.at[14])
    for u, dev in ((0, up), (1, down)):
        add(*mid_sum(y2, u, 0), to=one_unit(y2, u))
        pass_on(one_unit(y2, u), q1.at[u], rr.at[18 + u], dev)
    arrived(qx.at[1], rr.at[15])
    add(*mid_sum(yp, 1, 1), to=one_unit(yp, 1))
    pass_on(one_unit(yp, 1), q23.at[0, 1], rr.at[21], up)
    arrived(qx.at[2], rr.at[16])
    add(*mid_sum(ym, 0, 2), to=one_unit(ym, 0))
    pass_on(one_unit(ym, 0), q23.at[1, 0], rr.at[22], down)
    l_m = [load(first.at[:, half(h)], acc.at[unit(y2, h, 1, 0)], 7 + h) for h in range(2)]
    l_v = [load(second.at[:, half(h)], acc.at[unit(y2, h, 1, 1)], 9 + h) for h in range(2)]
    arrived(q1.at[0], rr.at[18])
    add(*mid_sum(yp, 0, 1), q1.at[0], to=one_unit(yp, 0))
    pass_on(one_unit(yp, 0), q23.at[0, 0], rr.at[20], up)
    arrived(q1.at[1], rr.at[19])
    add(*mid_sum(ym, 1, 2), q1.at[1], to=one_unit(ym, 1))
    pass_on(one_unit(ym, 1), q23.at[1, 1], rr.at[23], down)
    along_rest.end(rx.at[1], rr.at[13])
    arrived(qx.at[3], rr.at[17])
    arrived(rx.at[0], rr.at[12])
    add(at_unit(y, xh), 2 * OWN, rest, rx.at[0])
    for u in range(2):
        arrived(q23.at[0, u], rr.at[20 + u])
        arrived(q23.at[1, u], rr.at[22 + u])
        add(*mid_sum(y, u, 3), q23.at[0, u], q23.at[1, u])
    arrived(rx.at[1], rr.at[13])
    add(at_unit(y, xh), 2 * OWN, near, rx.at[1])

    r_sends.append(send(acc.at[pl.ds(al(at_unit(y, xh, 1 - c), 32), OWN)], gx, rr.at[24], sib))

    @pl.loop(0, 256 // 32)
    def _(r):
        mo[pl.ds(al(r * 32, 32), 32), :] = jnp.zeros((32, FEAT), BF16)

    for copy in l_m + l_v:
        copy.wait()
    shift = (d % 4) * 32
    stores = []

    def adam(which, gradient, start):
        @pl.loop(0, OWN // 16)
        def _(r):
            here = pl.ds(al(r * 16, 16), 16)
            cols = half(which)
            at_m = pl.ds(al(at_unit(y2, which, 0) + r * 16, 16), 16)
            at_v = pl.ds(al(at_unit(y2, which, 1) + r * 16, 16), 16)
            g = gradient[pl.ds(al(start + r * 16, 16), 16), :]
            params = mst[here, cols]
            m = FIRST_DECAY * acc[at_m, :] + (1.0 - FIRST_DECAY) * g
            v = SECOND_DECAY * acc[at_v, :] + (1.0 - SECOND_DECAY) * g * g
            acc[at_m, :] = m
            acc[at_v, :] = v
            direction = m / FIRST_CORRECTION / (jnp.sqrt(v / SECOND_CORRECTION) + EPSILON)
            new = params - LEARN_RATE * (direction + WEIGHT_DECAY * params)
            mst[here, cols] = new
            mo[pl.ds(al(shift + r * 16, 16), 16), cols] = new.astype(BF16)

        n = 11 if which is c else 14
        stores.append(load(mst.at[:, half(which)], out_p.at[:, half(which)], n))
        stores.append(load(acc.at[unit(y2, which, 1, 0)], out_m.at[:, half(which)], n + 1))
        stores.append(load(acc.at[unit(y2, which, 1, 1)], out_v.at[:, half(which)], n + 2))

    adam(c, acc, at_unit(y, xh, c))
    arrived(gx, rr.at[24])
    adam(1 - c, gx, 0)

    l_ni.wait()
    for i in range(1, 16):
        e = (d - i + 16) % 16
        arrived(niw.at[pl.ds(al((e % 2) * 256 + (e // 2) * 32, 32), 32)], nr.at[i])
    c_sends = []
    for q in range(4):
        cols = pl.ds(q * QUART, QUART)
        gv[pl.ds(0, 256), cols] = jnp.dot(
            niw[pl.ds(al((1 - c) * 256, 256), 256), :],
            mo[pl.ds(0, 256), cols],
            preferred_element_type=F32,
        ).astype(BF16)
        c_sends.append(send(gv.at[pl.ds(0, 256), cols], cz.at[:, cols], zr.at[q], sib))
    for q in range(4):
        cols = pl.ds(q * QUART, QUART)
        total = jnp.dot(
            niw[pl.ds(al(c * 256, 256), 256), :],
            mo[pl.ds(0, 256), cols],
            preferred_element_type=F32,
        )
        arrived(cz.at[:, cols], zr.at[q])
        gv[pl.ds(256, 256), cols] = (total + cz[:, cols].astype(F32)).astype(BF16)
    for i in range(1, 8):
        e = (k + i) % 8
        c_sends.append(
            send(
                gv.at[pl.ds(al(256 + e * 32, 32), 32)],
                cr.at[i],
                cs.at[i],
                (s, e * 2 + c),
            )
        )
    for i in range(1, 8):
        arrived(cr.at[i], cs.at[i])

    @pl.loop(0, 2)
    def _(r):
        here = pl.ds(al(r * 16, 16), 16)
        for q in range(4):
            cols = pl.ds(q * QUART, QUART)
            total = gv[pl.ds(al(256 + k * 32 + r * 16, 16), 16), cols].astype(F32)
            for i in range(1, 8):
                total += cr[i, here, cols].astype(F32)
            res[here, cols] = total.astype(BF16)

    stores.append(load(res, out_c, 17))
    for copy in stores:
        copy.wait()
    for copy in n_sends + r_sends + c_sends:
        copy.wait_send()

    @pl.when(s > 0)
    def _():
        for copy in p_sends:
            copy.wait_send()


def settle_kernel(*refs):
    count = len(refs) // 4
    sources, targets, held, sems = (refs[i * count : (i + 1) * count] for i in range(4))
    taken = [pltpu.make_async_copy(a, v, m.at[0]) for a, v, m in zip(sources, held, sems)]
    given = [pltpu.make_async_copy(v, b, m.at[1]) for v, b, m in zip(held, targets, sems)]
    for copy in taken:
        copy.start()
    for copy, onward in zip(taken, given):
        copy.wait()
        onward.start()
    for copy in given:
        copy.wait()


def settle(*values):
    anywhere = pl.BlockSpec(memory_space=pl.ANY)
    return pl.pallas_call(
        settle_kernel,
        out_shape=tuple(jax.ShapeDtypeStruct(v.shape, v.dtype) for v in values),
        in_specs=[anywhere] * len(values),
        out_specs=[anywhere] * len(values),
        scratch_shapes=[pltpu.VMEM(v.shape, v.dtype) for v in values]
        + [pltpu.SemaphoreType.DMA((2,)) for _ in values],
        name="settle",
    )(*values)


def step(master, first, second, xo, xa, grads, wo, wa, ni):
    vm = pltpu.VMEM
    dma = pltpu.SemaphoreType.DMA
    anywhere = pl.BlockSpec(memory_space=pl.ANY)
    shape = jax.ShapeDtypeStruct
    flat = (ROWS, FEAT)
    new = pl.pallas_call(
        kernel,
        out_shape=(
            shape((OWN, FEAT), F32),
            shape((OWN, FEAT), F32),
            shape((OWN, FEAT), F32),
            shape((32, FEAT), BF16),
        ),
        in_specs=[anywhere] * 9,
        out_specs=[anywhere] * 4,
        scratch_shapes=[
            vm((FEAT, FEAT), BF16),
            vm(flat, BF16),
            vm((ROWS, HALF), BF16),
            vm((2, ROWS, FEAT), BF16),
            vm((2, ROWS, FEAT), BF16),
            vm((FEAT, HALF), F32),
            vm(flat, BF16),
            vm((TOK, FEAT), jnp.int32),
            vm((2, TOK, HALF), jnp.int32),
            vm((OWN, FEAT), F32),
            vm((4, ROWS, QUART), BF16),
            vm((2, 2, ROWS, QUART), BF16),
            vm((512, 256), BF16),
            vm((2, 2 * OWN, PAIR), BF16),
            vm((2, 2, 2 * OWN, PAIR), BF16),
            vm((2, 2 * OWN, PAIR), BF16),
            vm((2, 2, 2 * OWN, PAIR), BF16),
            vm((2, 2 * OWN, PAIR), BF16),
            vm((4, 2 * OWN, MIDS), BF16),
            vm((2, OWN, MIDS), BF16),
            vm((2, 2, OWN, MIDS), BF16),
            vm((OWN, HALF), F32),
            vm((256, FEAT), BF16),
            vm((8, 32, FEAT), BF16),
            vm((32, FEAT), BF16),
            dma((18,)),
            dma((112,)),
            dma((9,)),
            dma((10,)),
            dma((4,)),
            dma((16,)),
            dma((2, 2, 2, 2)),
            dma((25,)),
            dma((4,)),
            dma((8,)),
        ],
        compiler_params=pltpu.CompilerParams(
            collective_id=0, has_side_effects=True, vmem_limit_bytes=67043328
        ),
        name="section_step",
    )(
        master[0],
        first[0],
        second[0],
        xo[0].reshape(flat),
        xa[0].reshape(flat),
        grads[0].reshape(flat),
        wo[0],
        wa[0],
        ni[0],
    )
    return tuple(value[None] for value in settle(*new))


def solution(mesh):
    row = P("section", "dp", None)
    deep = P("section", None, "dp", None)
    return jax.shard_map(
        step,
        mesh=mesh,
        in_specs=(row, row, row, deep, deep, deep, row, row, row),
        out_specs=(row, row, row, row),
        check_vma=False,
    )
```

```python
import jax
import jax.numpy as jnp
from jax import lax
from jax.experimental import pallas as pl
from jax.experimental.pallas import tpu as pltpu
from jax.sharding import PartitionSpec as P

LEAK_RATE = 0.5
LEARN_RATE = 0.002
FIRST_DECAY = 0.9
SECOND_DECAY = 0.95
EPSILON = 1e-08
WEIGHT_DECAY = 0.1
FIRST_CORRECTION = 1.0 - 0.9**10
SECOND_CORRECTION = 1.0 - 0.95**10

MESH = pl.DeviceIdType.MESH
F32, BF16 = jnp.float32, jnp.bfloat16
FEAT, HALF, QUART, OWN = 2560, 1280, 640, 160
ROWS, TOK, STEPS = 512, 128, 4
PART, MID = 256, 128
PAIR, MIDS = 2 * PART, 2 * MID


def al(value, by):
    return pl.multiple_of(value, by)


def kernel(
    master, first, second, xo, xa, grads, wo, wa, ni,
    out_p, out_m, out_v, out_c,
    wb, mo, mos, xov, xav, acc, gv, wov, wav, mst, outb, rcv, niw,
    n1, n23, r1, r23, rx, qx, q1, q23, gx, cz, cr, res,
    loc, snd, wr, ws, xs, nr, pr, rr, zr, cs,
):
    s, d = lax.axis_index("section"), lax.axis_index("dp")
    y, xh, c, k = d // 4, (d // 2) % 2, d % 2, d // 2
    yp, ym, y2 = (y + 1) % 4, (y + 3) % 4, (y + 2) % 4

    def index(y_, xh_, c_):
        return (y_ * 2 + xh_) * 2 + c_

    sib, xp = (s, index(y, xh, 1 - c)), (s, index(y, 1 - xh, c))
    up, down = (s, index(yp, xh, c)), (s, index(ym, xh, c))
    used = [0]

    def send(src, dst, sem, dev):
        copy = pltpu.make_async_remote_copy(
            src_ref=src, dst_ref=dst, send_sem=snd.at[used[0]], recv_sem=sem,
            device_id=dev, device_id_type=MESH,
        )
        used[0] += 1
        copy.start()
        return copy

    def arrived(dst, sem):
        pltpu.make_async_remote_copy(
            src_ref=dst, dst_ref=dst, send_sem=snd.at[0], recv_sem=sem,
            device_id=sib, device_id_type=MESH,
        ).wait_recv()

    def load(src, dst, i):
        copy = pltpu.make_async_copy(src, dst, loc.at[i])
        copy.start()
        return copy

    def owner(y_, xh_, c_, part=0, rows=OWN):
        return wb.at[pl.ds(al(index(y_, xh_, c_) * OWN + part, 16), rows)]

    def half(which):
        return pl.ds(al(which * HALF, 128), HALF)

    l_mst = load(master, mst, 0)
    l_g = load(grads, gv, 1)
    l_wo = load(wo, wov, 2)
    l_xo = load(xo, xov.at[c], 3)
    l_xa = load(xa, xav.at[c], 4)
    l_wa = load(wa.at[:, half(c)], wav.at[c], 5)

    def base(e):
        return al(e * OWN - (e % 4) * 32, 128)

    l_ni = load(
        ni.at[:, pl.ds(base(d), 256)], niw.at[pl.ds(al(c * 256 + k * 32, 32), 32)], 6
    )

    barrier = pltpu.get_barrier_semaphore()
    for i in range(1, 16):
        pl.semaphore_signal(barrier, inc=1, device_id=(s, (d + i) % 16), device_id_type=MESH)

    @pl.when(s > 0)
    def _():
        for h in range(2):
            pl.semaphore_signal(barrier, inc=1, device_id=(s - 1, k * 2 + h), device_id_type=MESH)

    @pl.when(s < 7)
    def _():
        for h in range(2):
            pl.semaphore_signal(barrier, inc=1, device_id=(s + 1, k * 2 + h), device_id_type=MESH)

    l_mst.wait()

    @pl.loop(0, OWN // 16)
    def _(r):
        wb[pl.ds(al(d * OWN + r * 16, 16), 16), :] = mst[pl.ds(al(r * 16, 16), 16), :].astype(BF16)

    pl.semaphore_wait(barrier, 15 + 2 * jnp.minimum(s, 1) + 2 * jnp.minimum(7 - s, 1))

    mine = owner(y, xh, c)
    w_sends = [
        send(mine, mine, wr.at[0], xp),
        send(mine, mine, wr.at[1], up),
        send(mine, mine, wr.at[2], down),
        send(mine, mine, ws.at[0], sib),
    ]
    x_sends = [
        send(xo, xov.at[c], xs.at[0], sib),
        send(wa.at[:, half(1 - c)], wav.at[c], xs.at[1], sib),
    ]
    l_g.wait()
    l_wo.wait()

    @pl.loop(0, TOK // 16)
    def _(r):
        for q in range(4):
            cols = pl.ds(q * QUART, QUART)
            bits = wov[pl.ds(al(r * 16, 16), 16), cols]
            carry = jnp.zeros((16, QUART), F32)
            for t in reversed(range(STEPS)):
                rows = pl.ds(al(t * TOK + r * 16, 16), 16)
                window = ((bits >> t) & 1).astype(F32)
                carry = window * gv[rows, cols].astype(F32) + LEAK_RATE * carry
                mo[rows, cols] = carry.astype(BF16)

    x_sends.append(send(mo.at[:, half(1 - c)], mos, xs.at[3], sib))
    x_sends.append(send(xa, xav.at[c], xs.at[2], sib))

    p_sends = []

    parts = ((xh * 384, 256), ((1 - xh) * 256, 384))

    def outgoing(b, n, part):
        begin, width = parts[part]
        cols = pl.ds(al(begin, 128), width)
        wide = pl.ds(al(b * QUART + begin, 128), width)
        for h in (1, 0):
            rows = pl.ds(h * 256, 256)
            through = lax.dot_general(
                mo[rows, :], wb[wide, :], (((1,), (1,)), ((), ())), preferred_element_type=F32
            )
            outb[n, rows, cols] = (gv[rows, wide].astype(F32) + through).astype(BF16)
            copy = pltpu.make_async_remote_copy(
                src_ref=outb.at[n, rows, cols],
                dst_ref=rcv.at[c, b % 2, rows, cols],
                send_sem=snd.at[used[0]],
                recv_sem=pr.at[c, b % 2, part, h],
                device_id=(s - 1, k * 2 + b // 2),
                device_id_type=MESH,
            )
            used[0] += 1
            p_sends.append(copy)
            pl.when(s > 0)(copy.start)

    def relay(kind, piece, *targets):
        arrived(piece, wr.at[kind])
        for region, sem, dev in targets:
            w_sends.append(send(region, region, sem, dev))

    arrived(owner(y, xh, 1 - c), ws.at[0])
    outgoing(y, 0, 0)
    piece = owner(ym, xh, c)
    relay(1, piece, (owner(ym, xh, c, 0, 80), wr.at[5], up))
    piece = owner(yp, xh, c)
    relay(2, piece, (owner(yp, xh, c, 80, 80), wr.at[6], down))
    piece = owner(y, 1 - xh, c)
    relay(0, piece, (piece, ws.at[1], sib), (piece, wr.at[3], up), (piece, wr.at[4], down))
    for piece, i in ((owner(ym, xh, c), 2), (owner(yp, xh, c), 3)):
        w_sends.append(send(piece, piece, ws.at[i], sib))
    arrived(owner(y, 1 - xh, 1 - c), ws.at[1])
    outgoing(y, 0, 1)
    arrived(owner(ym, xh, 1 - c), ws.at[2])
    outgoing(ym, 1, 0)
    arrived(owner(yp, xh, 1 - c), ws.at[3])
    outgoing(yp, 2, 0)

    across = (((0,), (0,)), ((), ()))
    l_xo.wait()
    arrived(xov.at[1 - c], xs.at[0])
    arrived(mos, xs.at[3])

    @pl.loop(0, 4)
    def _(b):
        rows = pl.ds(al(b * QUART, 128), QUART)
        for j in range(2):
            acc[rows, pl.ds(j * QUART, QUART)] = lax.dot_general(
                xov[c, :, rows],
                mo[:, pl.ds(al(c * HALF + j * QUART, 128), QUART)],
                across,
                preferred_element_type=F32,
            ) + lax.dot_general(
                xov[1 - c, :, rows],
                mos[:, pl.ds(j * QUART, QUART)],
                across,
                preferred_element_type=F32,
            )

    def far_block(xh_, n):
        for i in range(2):
            piece = owner(y2, xh_, c, 80 * i, 80)
            relay(5 + 2 * n + i, piece, (piece, ws.at[6 + 2 * n + i], sib))
        for i in range(2):
            arrived(owner(y2, xh_, 1 - c, 80 * i, 80), ws.at[6 + 2 * n + i])
        outgoing(y2, 3, n)

    far_block(xh, 0)
    piece = owner(ym, 1 - xh, c)
    relay(3, piece, (owner(ym, 1 - xh, c, 0, 80), wr.at[7], up), (piece, ws.at[4], sib))
    piece = owner(yp, 1 - xh, c)
    relay(4, piece, (owner(yp, 1 - xh, c, 80, 80), wr.at[8], down), (piece, ws.at[5], sib))
    arrived(owner(ym, 1 - xh, 1 - c), ws.at[4])
    outgoing(ym, 1, 1)
    arrived(owner(yp, 1 - xh, 1 - c), ws.at[5])
    outgoing(yp, 2, 1)

    l_xa.wait()
    arrived(xav.at[1 - c], xs.at[2])
    l_wa.wait()
    arrived(wav.at[1 - c], xs.at[1])

    def arriving(part):
        begin, width = parts[part]
        cols = pl.ds(al(begin, 128), width)
        for j in range(2):
            for cc in range(2):
                for h in (1, 0):
                    arrived(rcv.at[cc, j, pl.ds(h * 256, 256), cols], pr.at[cc, j, part, h])

                @pl.loop(0, TOK // 16)
                def _(r, cc=cc, j=j):
                    here = pl.ds(al(r * 16, 16), 16)
                    bits = wav[cc, here, pl.ds(al(j * QUART + begin, 128), width)]
                    carry = jnp.zeros((16, width), F32)
                    for t in reversed(range(STEPS)):
                        rows = pl.ds(al(t * TOK + r * 16, 16), 16)
                        window = ((bits >> t) & 1).astype(F32)
                        carry = window * rcv[cc, j, rows, cols].astype(F32) + LEAK_RATE * carry
                        rcv[cc, j, rows, cols] = carry.astype(BF16)

    def more(b, part):
        begin, width = parts[part]
        rows = pl.ds(al(b * QUART, 128), QUART)
        cols = pl.ds(al(begin, 128), width)

        @pl.when(s < 7)
        def _():
            for j in range(2):
                acc[rows, pl.ds(al(j * QUART + begin, 128), width)] += lax.dot_general(
                    xav[0, :, rows], rcv[0, j, :, cols], across, preferred_element_type=F32
                ) + lax.dot_general(
                    xav[1, :, rows], rcv[1, j, :, cols], across, preferred_element_type=F32
                )

    near, rest, mid = (xh * 384, PART), ((1 - xh) * 384, PART), (PART, MID)
    r_sends = []

    def at_unit(y_, xh_, c_=0):
        return index(y_, xh_, c_) * OWN

    def unit(y_, xh_, n=2, first_=0):
        return pl.ds(al(at_unit(y_, xh_, first_), 32), n * OWN)

    def add(start, count, group, *terms, to=None):
        begin, width = group
        height = 32

        @pl.loop(0, count // height)
        def _(r):
            rows = pl.ds(al(start + r * height, 32), height)
            here = pl.ds(al(r * height, 32), height)
            for j in range(2):
                cols = pl.ds(al(j * QUART + begin, 128), width)
                side = pl.ds(j * width, width)
                total = acc[rows, cols]
                for term in terms:
                    total += term[here, side].astype(F32)
                if to is None:
                    acc[rows, cols] = total
                else:
                    to[here, side] = total.astype(BF16)

    def pass_on(src, dst, sem, dev):
        r_sends.append(send(src, dst, sem, dev))

    class AlongY:
        def __init__(self, group, place, one, two, sems):
            self.group, self.place, self.one, self.two, self.sems = group, place, one, two, sems

        def begin(self, b):
            for xh_ in range(2):
                keep = (b is yp and xh_ == 0) or (b is ym and xh_ == 1) or b is y
                if keep:
                    continue
                ref = self.place(b, xh_)
                add(at_unit(b, xh_), 2 * OWN, self.group, to=ref)
                if b is y2:
                    pass_on(ref, self.one.at[xh_], rr.at[self.sems + xh_], (up, down)[xh_])
                elif b is yp:
                    pass_on(ref, self.two.at[0, 1], rr.at[self.sems + 3], up)
                else:
                    pass_on(ref, self.two.at[1, 0], rr.at[self.sems + 4], down)

        def middle(self):
            for xh_, b, dev, sem in ((0, yp, up, 2), (1, ym, down, 5)):
                arrived(self.one.at[xh_], rr.at[self.sems + xh_])
                ref = self.place(b, xh_)
                add(at_unit(b, xh_), 2 * OWN, self.group, self.one.at[xh_], to=ref)
                pass_on(ref, self.two.at[xh_, xh_], rr.at[self.sems + sem], dev)

        def end(self, there, sem):
            for i, h, sem_ in ((0, 1, 3), (1, 0, 4), (0, 0, 2), (1, 1, 5)):
                arrived(self.two.at[i, h], rr.at[self.sems + sem_])
            other = self.place(y, 1 - xh)
            add(
                at_unit(y, 1 - xh), 2 * OWN, self.group,
                self.two.at[0, 1 - xh], self.two.at[1, 1 - xh], to=other,
            )
            pass_on(other, there, sem, xp)
            add(at_unit(y, xh), 2 * OWN, self.group, self.two.at[0, xh], self.two.at[1, xh])

    def near_place(b, xh_):
        chip = b * 2 + xh_
        return xov.at[chip // 5, pl.ds(0, 2 * OWN), pl.ds(al((chip % 5) * PAIR, 128), PAIR)]

    def rest_place(b, xh_):
        return wb.at[unit(b, xh_), pl.ds(0, PAIR)]

    along_near = AlongY(near, near_place, n1, n23, 0)
    along_rest = AlongY(rest, rest_place, r1, r23, 6)

    pl.when(s < 7)(lambda: arriving(0))
    for b in (y2, yp, ym, y):
        more(b, 0)
        along_near.begin(b)

    far_block(1 - xh, 1)
    along_near.middle()
    for copy in w_sends + x_sends:
        copy.wait_send()
    pl.when(s < 7)(lambda: arriving(1))
    mcol = pl.ds(PAIR, MIDS)

    for n, b in enumerate((y2, yp, ym, y)):
        more(b, 1)
        along_rest.begin(b)
        ref = wb.at[unit(b, 1 - xh), mcol]
        add(at_unit(b, 1 - xh), 2 * OWN, mid, to=ref)
        pass_on(ref, qx.at[n], rr.at[14 + n], xp)
    along_rest.middle()
    along_near.end(rx.at[0], rr.at[12])
    n_sends = []
    for i in range(1, 16):
        e = (d + i) % 16
        n_sends.append(
            send(
                ni.at[:, pl.ds(base(e), 256)],
                niw.at[pl.ds(al(c * 256 + k * 32, 32), 32)],
                nr.at[i],
                (s, e),
            )
        )


    def one_unit(y_, u):
        return wb.at[unit(y_, xh, 1, u), mcol]

    def mid_sum(y_, u, n):
        return at_unit(y_, xh, u), OWN, mid, qx.at[n, pl.ds(u * OWN, OWN)]

    arrived(qx.at[0], rr.at[14])
    for u, dev in ((0, up), (1, down)):
        add(*mid_sum(y2, u, 0), to=one_unit(y2, u))
        pass_on(one_unit(y2, u), q1.at[u], rr.at[18 + u], dev)
    arrived(qx.at[1], rr.at[15])
    add(*mid_sum(yp, 1, 1), to=one_unit(yp, 1))
    pass_on(one_unit(yp, 1), q23.at[0, 1], rr.at[21], up)
    arrived(qx.at[2], rr.at[16])
    add(*mid_sum(ym, 0, 2), to=one_unit(ym, 0))
    pass_on(one_unit(ym, 0), q23.at[1, 0], rr.at[22], down)
    l_m = [load(first.at[:, half(h)], acc.at[unit(y2, h, 1, 0)], 7 + h) for h in range(2)]
    l_v = [load(second.at[:, half(h)], acc.at[unit(y2, h, 1, 1)], 9 + h) for h in range(2)]
    along_rest.end(rx.at[1], rr.at[13])
    arrived(q1.at[0], rr.at[18])
    add(*mid_sum(yp, 0, 1), q1.at[0], to=one_unit(yp, 0))
    pass_on(one_unit(yp, 0), q23.at[0, 0], rr.at[20], up)
    arrived(q1.at[1], rr.at[19])
    add(*mid_sum(ym, 1, 2), q1.at[1], to=one_unit(ym, 1))
    pass_on(one_unit(ym, 1), q23.at[1, 1], rr.at[23], down)
    arrived(qx.at[3], rr.at[17])
    arrived(rx.at[0], rr.at[12])
    add(at_unit(y, xh), 2 * OWN, rest, rx.at[0])
    for u in range(2):
        arrived(q23.at[0, u], rr.at[20 + u])
        arrived(q23.at[1, u], rr.at[22 + u])
        add(*mid_sum(y, u, 3), q23.at[0, u], q23.at[1, u])
    arrived(rx.at[1], rr.at[13])
    add(at_unit(y, xh), 2 * OWN, near, rx.at[1])

    r_sends.append(send(acc.at[pl.ds(al(at_unit(y, xh, 1 - c), 32), OWN)], gx, rr.at[24], sib))

    @pl.loop(0, 256 // 32)
    def _(r):
        mo[pl.ds(al(r * 32, 32), 32), :] = jnp.zeros((32, FEAT), BF16)

    for copy in l_m + l_v:
        copy.wait()
    shift = (d % 4) * 32
    stores = []

    def adam(which, gradient, start):
        @pl.loop(0, OWN // 16)
        def _(r):
            here = pl.ds(al(r * 16, 16), 16)
            cols = half(which)
            at_m = pl.ds(al(at_unit(y2, which, 0) + r * 16, 16), 16)
            at_v = pl.ds(al(at_unit(y2, which, 1) + r * 16, 16), 16)
            g = gradient[pl.ds(al(start + r * 16, 16), 16), :]
            params = mst[here, cols]
            m = FIRST_DECAY * acc[at_m, :] + (1.0 - FIRST_DECAY) * g
            v = SECOND_DECAY * acc[at_v, :] + (1.0 - SECOND_DECAY) * g * g
            acc[at_m, :] = m
            acc[at_v, :] = v
            direction = m / FIRST_CORRECTION / (jnp.sqrt(v / SECOND_CORRECTION) + EPSILON)
            new = params - LEARN_RATE * (direction + WEIGHT_DECAY * params)
            mst[here, cols] = new
            mo[pl.ds(al(shift + r * 16, 16), 16), cols] = new.astype(BF16)

        n = 11 if which is c else 14
        stores.append(load(mst.at[:, half(which)], out_p.at[:, half(which)], n))
        stores.append(load(acc.at[unit(y2, which, 1, 0)], out_m.at[:, half(which)], n + 1))
        stores.append(load(acc.at[unit(y2, which, 1, 1)], out_v.at[:, half(which)], n + 2))

    l_ni.wait()
    for i in range(1, 16):
        e = (d - i + 16) % 16
        arrived(niw.at[pl.ds(al((e % 2) * 256 + (e // 2) * 32, 32), 32)], nr.at[i])
    c_sends = []

    def product(c_, cols):
        return jnp.dot(
            niw[pl.ds(al(c_ * 256, 256), 256), :],
            mo[pl.ds(0, 256), cols],
            preferred_element_type=F32,
        )

    order = [(h, q, pl.ds(al(which * HALF + q * QUART, 128), QUART))
             for h, which in enumerate((c, 1 - c)) for q in range(2)]
    for turn, (which, gradient, start) in enumerate(((c, acc, at_unit(y, xh, c)), (1 - c, gx, 0))):
        if turn == 1:
            arrived(gx, rr.at[24])
        adam(which, gradient, start)
        for h, q, cols in order:
            if h == turn:
                gv[pl.ds(0, 256), cols] = product(1 - c, cols).astype(BF16)
                c_sends.append(
                    send(gv.at[pl.ds(0, 256), cols], cz.at[:, cols], zr.at[(1 - h) * 2 + q], sib)
                )
    for h, q, cols in reversed(order):
        total = product(c, cols)
        arrived(cz.at[:, cols], zr.at[h * 2 + q])
        gv[pl.ds(256, 256), cols] = (total + cz[:, cols].astype(F32)).astype(BF16)
        for i in range(1, 8):
            e = (k + i) % 8
            c_sends.append(
                send(
                    gv.at[pl.ds(al(256 + e * 32, 32), 32), cols],
                    cr.at[i, :, cols],
                    cs.at[i, h * 2 + q],
                    (s, e * 2 + c),
                )
            )
    for h, q, cols in reversed(order):
        for i in range(1, 8):
            arrived(cr.at[i, :, cols], cs.at[i, h * 2 + q])

    @pl.loop(0, 2)
    def _(r):
        here = pl.ds(al(r * 16, 16), 16)
        for q in range(4):
            cols = pl.ds(q * QUART, QUART)
            total = gv[pl.ds(al(256 + k * 32 + r * 16, 16), 16), cols].astype(F32)
            for i in range(1, 8):
                total += cr[i, here, cols].astype(F32)
            res[here, cols] = total.astype(BF16)

    stores.append(load(res, out_c, 17))
    for copy in stores:
        copy.wait()
    for copy in n_sends + r_sends + c_sends:
        copy.wait_send()

    @pl.when(s > 0)
    def _():
        for copy in p_sends:
            copy.wait_send()


def settle_kernel(*refs):
    count = len(refs) // 4
    sources, targets, held, sems = (refs[i * count : (i + 1) * count] for i in range(4))
    taken = [pltpu.make_async_copy(a, v, m.at[0]) for a, v, m in zip(sources, held, sems)]
    given = [pltpu.make_async_copy(v, b, m.at[1]) for v, b, m in zip(held, targets, sems)]
    for copy in taken:
        copy.start()
    for copy, onward in zip(taken, given):
        copy.wait()
        onward.start()
    for copy in given:
        copy.wait()


def settle(*values):
    anywhere = pl.BlockSpec(memory_space=pl.ANY)
    return pl.pallas_call(
        settle_kernel,
        out_shape=tuple(jax.ShapeDtypeStruct(v.shape, v.dtype) for v in values),
        in_specs=[anywhere] * len(values),
        out_specs=[anywhere] * len(values),
        scratch_shapes=[pltpu.VMEM(v.shape, v.dtype) for v in values]
        + [pltpu.SemaphoreType.DMA((2,)) for _ in values],
        name="settle",
    )(*values)


def step(master, first, second, xo, xa, grads, wo, wa, ni):
    vm = pltpu.VMEM
    dma = pltpu.SemaphoreType.DMA
    anywhere = pl.BlockSpec(memory_space=pl.ANY)
    shape = jax.ShapeDtypeStruct
    flat = (ROWS, FEAT)
    new = pl.pallas_call(
        kernel,
        out_shape=(
            shape((OWN, FEAT), F32),
            shape((OWN, FEAT), F32),
            shape((OWN, FEAT), F32),
            shape((32, FEAT), BF16),
        ),
        in_specs=[anywhere] * 9,
        out_specs=[anywhere] * 4,
        scratch_shapes=[
            vm((FEAT, FEAT), BF16),
            vm(flat, BF16),
            vm((ROWS, HALF), BF16),
            vm((2, ROWS, FEAT), BF16),
            vm((2, ROWS, FEAT), BF16),
            vm((FEAT, HALF), F32),
            vm(flat, BF16),
            vm((TOK, FEAT), jnp.int32),
            vm((2, TOK, HALF), jnp.int32),
            vm((OWN, FEAT), F32),
            vm((4, ROWS, QUART), BF16),
            vm((2, 2, ROWS, QUART), BF16),
            vm((512, 256), BF16),
            vm((2, 2 * OWN, PAIR), BF16),
            vm((2, 2, 2 * OWN, PAIR), BF16),
            vm((2, 2 * OWN, PAIR), BF16),
            vm((2, 2, 2 * OWN, PAIR), BF16),
            vm((2, 2 * OWN, PAIR), BF16),
            vm((4, 2 * OWN, MIDS), BF16),
            vm((2, OWN, MIDS), BF16),
            vm((2, 2, OWN, MIDS), BF16),
            vm((OWN, HALF), F32),
            vm((256, FEAT), BF16),
            vm((8, 32, FEAT), BF16),
            vm((32, FEAT), BF16),
            dma((18,)),
            dma((160,)),
            dma((9,)),
            dma((10,)),
            dma((4,)),
            dma((16,)),
            dma((2, 2, 2, 2)),
            dma((25,)),
            dma((4,)),
            dma((8, 4)),
        ],
        compiler_params=pltpu.CompilerParams(
            collective_id=0, has_side_effects=True, vmem_limit_bytes=67043328
        ),
        name="section_step",
    )(
        master[0],
        first[0],
        second[0],
        xo[0].reshape(flat),
        xa[0].reshape(flat),
        grads[0].reshape(flat),
        wo[0],
        wa[0],
        ni[0],
    )
    return tuple(value[None] for value in settle(*new))


def solution(mesh):
    row = P("section", "dp", None)
    deep = P("section", None, "dp", None)
    return jax.shard_map(
        step,
        mesh=mesh,
        in_specs=(row, row, row, deep, deep, deep, row, row, row),
        out_specs=(row, row, row, row),
        check_vma=False,
    )
```

```python
import jax
import jax.numpy as jnp
from jax import lax
from jax.experimental import pallas as pl
from jax.experimental.pallas import tpu as pltpu
from jax.sharding import PartitionSpec as P

LEAK_RATE = 0.5
LEARN_RATE = 0.002
FIRST_DECAY = 0.9
SECOND_DECAY = 0.95
EPSILON = 1e-08
WEIGHT_DECAY = 0.1
FIRST_CORRECTION = 1.0 - 0.9**10
SECOND_CORRECTION = 1.0 - 0.95**10

MESH = pl.DeviceIdType.MESH
F32, BF16 = jnp.float32, jnp.bfloat16
FEAT, HALF, QUART, OWN = 2560, 1280, 640, 160
ROWS, TOK, STEPS = 512, 128, 4
PART, MID = 256, 128
PAIR, MIDS = 2 * PART, 2 * MID


def al(value, by):
    return pl.multiple_of(value, by)


def kernel(
    master, first, second, xo, xa, grads, wo, wa, ni,
    out_p, out_m, out_v, out_c,
    wb, mo, mos, xov, xav, acc, gv, wov, wav, mst, outb, rcv, niw,
    n1, n23, r1, r23, rx, qx, q1, q23, gx, cz, cr, res,
    loc, snd, wr, ws, xs, nr, pr, rr, zr, cs,
):
    s, d = lax.axis_index("section"), lax.axis_index("dp")
    y, xh, c, k = d // 4, (d // 2) % 2, d % 2, d // 2
    yp, ym, y2 = (y + 1) % 4, (y + 3) % 4, (y + 2) % 4

    def index(y_, xh_, c_):
        return (y_ * 2 + xh_) * 2 + c_

    sib, xp = (s, index(y, xh, 1 - c)), (s, index(y, 1 - xh, c))
    up, down = (s, index(yp, xh, c)), (s, index(ym, xh, c))
    used = [0]

    def send(src, dst, sem, dev):
        copy = pltpu.make_async_remote_copy(
            src_ref=src, dst_ref=dst, send_sem=snd.at[used[0]], recv_sem=sem,
            device_id=dev, device_id_type=MESH,
        )
        used[0] += 1
        copy.start()
        return copy

    def arrived(dst, sem):
        pltpu.make_async_remote_copy(
            src_ref=dst, dst_ref=dst, send_sem=snd.at[0], recv_sem=sem,
            device_id=sib, device_id_type=MESH,
        ).wait_recv()

    def load(src, dst, i):
        copy = pltpu.make_async_copy(src, dst, loc.at[i])
        copy.start()
        return copy

    def owner(y_, xh_, c_, part=0, rows=OWN):
        return wb.at[pl.ds(al(index(y_, xh_, c_) * OWN + part, 16), rows)]

    def half(which):
        return pl.ds(al(which * HALF, 128), HALF)

    l_mst = load(master, mst, 0)
    l_g = load(grads, gv, 1)
    l_wo = load(wo, wov, 2)
    l_xo = load(xo, xov.at[c], 3)
    l_xa = load(xa, xav.at[c], 4)
    l_wa = load(wa.at[:, half(c)], wav.at[c], 5)

    def base(e):
        return al(e * OWN - (e % 4) * 32, 128)

    l_ni = load(
        ni.at[:, pl.ds(base(d), 256)], niw.at[pl.ds(al(c * 256 + k * 32, 32), 32)], 6
    )

    barrier = pltpu.get_barrier_semaphore()
    for i in range(1, 16):
        pl.semaphore_signal(barrier, inc=1, device_id=(s, (d + i) % 16), device_id_type=MESH)

    @pl.when(s > 0)
    def _():
        for h in range(2):
            pl.semaphore_signal(barrier, inc=1, device_id=(s - 1, k * 2 + h), device_id_type=MESH)

    @pl.when(s < 7)
    def _():
        for h in range(2):
            pl.semaphore_signal(barrier, inc=1, device_id=(s + 1, k * 2 + h), device_id_type=MESH)

    l_mst.wait()

    @pl.loop(0, OWN // 16)
    def _(r):
        wb[pl.ds(al(d * OWN + r * 16, 16), 16), :] = mst[pl.ds(al(r * 16, 16), 16), :].astype(BF16)

    pl.semaphore_wait(barrier, 15 + 2 * jnp.minimum(s, 1) + 2 * jnp.minimum(7 - s, 1))

    mine = owner(y, xh, c)
    w_sends = [
        send(mine, mine, wr.at[0], xp),
        send(mine, mine, wr.at[1], up),
        send(mine, mine, wr.at[2], down),
        send(mine, mine, ws.at[0], sib),
    ]
    x_sends = [
        send(xo, xov.at[c], xs.at[0], sib),
        send(wa.at[:, half(1 - c)], wav.at[c], xs.at[1], sib),
    ]
    l_g.wait()
    l_wo.wait()

    @pl.loop(0, TOK // 16)
    def _(r):
        for q in range(4):
            cols = pl.ds(q * QUART, QUART)
            bits = wov[pl.ds(al(r * 16, 16), 16), cols]
            carry = jnp.zeros((16, QUART), F32)
            for t in reversed(range(STEPS)):
                rows = pl.ds(al(t * TOK + r * 16, 16), 16)
                window = ((bits >> t) & 1).astype(F32)
                carry = window * gv[rows, cols].astype(F32) + LEAK_RATE * carry
                mo[rows, cols] = carry.astype(BF16)

    x_sends.append(send(mo.at[:, half(1 - c)], mos, xs.at[3], sib))
    x_sends.append(send(xa, xav.at[c], xs.at[2], sib))

    p_sends = []

    parts = ((xh * 384, 256), ((1 - xh) * 256, 384))

    def outgoing(b, n, part):
        begin, width = parts[part]
        cols = pl.ds(al(begin, 128), width)
        wide = pl.ds(al(b * QUART + begin, 128), width)
        for h in (1, 0):
            rows = pl.ds(h * 256, 256)
            through = lax.dot_general(
                mo[rows, :], wb[wide, :], (((1,), (1,)), ((), ())), preferred_element_type=F32
            )
            outb[n, rows, cols] = (gv[rows, wide].astype(F32) + through).astype(BF16)
            copy = pltpu.make_async_remote_copy(
                src_ref=outb.at[n, rows, cols],
                dst_ref=rcv.at[c, b % 2, rows, cols],
                send_sem=snd.at[used[0]],
                recv_sem=pr.at[c, b % 2, part, h],
                device_id=(s - 1, k * 2 + b // 2),
                device_id_type=MESH,
            )
            used[0] += 1
            p_sends.append(copy)
            pl.when(s > 0)(copy.start)

    def relay(kind, piece, *targets):
        arrived(piece, wr.at[kind])
        for region, sem, dev in targets:
            w_sends.append(send(region, region, sem, dev))

    arrived(owner(y, xh, 1 - c), ws.at[0])
    outgoing(y, 0, 0)
    piece = owner(ym, xh, c)
    relay(1, piece, (owner(ym, xh, c, 0, 80), wr.at[5], up))
    piece = owner(yp, xh, c)
    relay(2, piece, (owner(yp, xh, c, 80, 80), wr.at[6], down))
    piece = owner(y, 1 - xh, c)
    relay(0, piece, (piece, ws.at[1], sib), (piece, wr.at[3], up), (piece, wr.at[4], down))
    for piece, i in ((owner(ym, xh, c), 2), (owner(yp, xh, c), 3)):
        w_sends.append(send(piece, piece, ws.at[i], sib))
    arrived(owner(y, 1 - xh, 1 - c), ws.at[1])
    outgoing(y, 0, 1)
    arrived(owner(ym, xh, 1 - c), ws.at[2])
    outgoing(ym, 1, 0)
    arrived(owner(yp, xh, 1 - c), ws.at[3])
    outgoing(yp, 2, 0)

    across = (((0,), (0,)), ((), ()))
    l_xo.wait()
    arrived(xov.at[1 - c], xs.at[0])
    arrived(mos, xs.at[3])

    @pl.loop(0, 4)
    def _(b):
        rows = pl.ds(al(b * QUART, 128), QUART)
        for j in range(2):
            acc[rows, pl.ds(j * QUART, QUART)] = lax.dot_general(
                xov[c, :, rows],
                mo[:, pl.ds(al(c * HALF + j * QUART, 128), QUART)],
                across,
                preferred_element_type=F32,
            ) + lax.dot_general(
                xov[1 - c, :, rows],
                mos[:, pl.ds(j * QUART, QUART)],
                across,
                preferred_element_type=F32,
            )

    def far_block(xh_, n):
        for i in range(2):
            piece = owner(y2, xh_, c, 80 * i, 80)
            relay(5 + 2 * n + i, piece, (piece, ws.at[6 + 2 * n + i], sib))
        for i in range(2):
            arrived(owner(y2, xh_, 1 - c, 80 * i, 80), ws.at[6 + 2 * n + i])
        outgoing(y2, 3, n)

    far_block(xh, 0)
    piece = owner(ym, 1 - xh, c)
    relay(3, piece, (owner(ym, 1 - xh, c, 0, 80), wr.at[7], up), (piece, ws.at[4], sib))
    piece = owner(yp, 1 - xh, c)
    relay(4, piece, (owner(yp, 1 - xh, c, 80, 80), wr.at[8], down), (piece, ws.at[5], sib))
    arrived(owner(ym, 1 - xh, 1 - c), ws.at[4])
    outgoing(ym, 1, 1)
    arrived(owner(yp, 1 - xh, 1 - c), ws.at[5])
    outgoing(yp, 2, 1)

    l_xa.wait()
    arrived(xav.at[1 - c], xs.at[2])
    l_wa.wait()
    arrived(wav.at[1 - c], xs.at[1])

    def arriving(part):
        begin, width = parts[part]
        cols = pl.ds(al(begin, 128), width)
        for j in range(2):
            for cc in range(2):
                for h in (1, 0):
                    arrived(rcv.at[cc, j, pl.ds(h * 256, 256), cols], pr.at[cc, j, part, h])

                @pl.loop(0, TOK // 16)
                def _(r, cc=cc, j=j):
                    here = pl.ds(al(r * 16, 16), 16)
                    bits = wav[cc, here, pl.ds(al(j * QUART + begin, 128), width)]
                    carry = jnp.zeros((16, width), F32)
                    for t in reversed(range(STEPS)):
                        rows = pl.ds(al(t * TOK + r * 16, 16), 16)
                        window = ((bits >> t) & 1).astype(F32)
                        carry = window * rcv[cc, j, rows, cols].astype(F32) + LEAK_RATE * carry
                        rcv[cc, j, rows, cols] = carry.astype(BF16)

    def more(b, part):
        begin, width = parts[part]
        rows = pl.ds(al(b * QUART, 128), QUART)
        cols = pl.ds(al(begin, 128), width)

        @pl.when(s < 7)
        def _():
            for j in range(2):
                acc[rows, pl.ds(al(j * QUART + begin, 128), width)] += lax.dot_general(
                    xav[0, :, rows], rcv[0, j, :, cols], across, preferred_element_type=F32
                ) + lax.dot_general(
                    xav[1, :, rows], rcv[1, j, :, cols], across, preferred_element_type=F32
                )

    near, rest, mid = (xh * 384, PART), ((1 - xh) * 384, PART), (PART, MID)
    r_sends = []

    def at_unit(y_, xh_, c_=0):
        return index(y_, xh_, c_) * OWN

    def unit(y_, xh_, n=2, first_=0):
        return pl.ds(al(at_unit(y_, xh_, first_), 32), n * OWN)

    def add(start, count, group, *terms, to=None):
        begin, width = group
        height = 32

        @pl.loop(0, count // height)
        def _(r):
            rows = pl.ds(al(start + r * height, 32), height)
            here = pl.ds(al(r * height, 32), height)
            for j in range(2):
                cols = pl.ds(al(j * QUART + begin, 128), width)
                side = pl.ds(j * width, width)
                total = acc[rows, cols]
                for term in terms:
                    total += term[here, side].astype(F32)
                if to is None:
                    acc[rows, cols] = total
                else:
                    to[here, side] = total.astype(BF16)

    def pass_on(src, dst, sem, dev):
        r_sends.append(send(src, dst, sem, dev))

    class AlongY:
        def __init__(self, group, place, one, two, sems):
            self.group, self.place, self.one, self.two, self.sems = group, place, one, two, sems

        def begin(self, b):
            for xh_ in range(2):
                keep = (b is yp and xh_ == 0) or (b is ym and xh_ == 1) or b is y
                if keep:
                    continue
                ref = self.place(b, xh_)
                add(at_unit(b, xh_), 2 * OWN, self.group, to=ref)
                if b is y2:
                    pass_on(ref, self.one.at[xh_], rr.at[self.sems + xh_], (up, down)[xh_])
                elif b is yp:
                    pass_on(ref, self.two.at[0, 1], rr.at[self.sems + 3], up)
                else:
                    pass_on(ref, self.two.at[1, 0], rr.at[self.sems + 4], down)

        def middle(self):
            for xh_, b, dev, sem in ((0, yp, up, 2), (1, ym, down, 5)):
                arrived(self.one.at[xh_], rr.at[self.sems + xh_])
                ref = self.place(b, xh_)
                add(at_unit(b, xh_), 2 * OWN, self.group, self.one.at[xh_], to=ref)
                pass_on(ref, self.two.at[xh_, xh_], rr.at[self.sems + sem], dev)

        def end(self, there, sem):
            for i, h, sem_ in ((0, 1, 3), (1, 0, 4), (0, 0, 2), (1, 1, 5)):
                arrived(self.two.at[i, h], rr.at[self.sems + sem_])
            other = self.place(y, 1 - xh)
            add(
                at_unit(y, 1 - xh), 2 * OWN, self.group,
                self.two.at[0, 1 - xh], self.two.at[1, 1 - xh], to=other,
            )
            pass_on(other, there, sem, xp)
            add(at_unit(y, xh), 2 * OWN, self.group, self.two.at[0, xh], self.two.at[1, xh])

    def near_place(b, xh_):
        chip = b * 2 + xh_
        return xov.at[chip // 5, pl.ds(0, 2 * OWN), pl.ds(al((chip % 5) * PAIR, 128), PAIR)]

    def rest_place(b, xh_):
        return wb.at[unit(b, xh_), pl.ds(0, PAIR)]

    along_near = AlongY(near, near_place, n1, n23, 0)
    along_rest = AlongY(rest, rest_place, r1, r23, 6)

    pl.when(s < 7)(lambda: arriving(0))
    for b in (y2, yp, ym, y):
        more(b, 0)
        along_near.begin(b)

    far_block(1 - xh, 1)
    along_near.middle()
    for copy in w_sends + x_sends:
        copy.wait_send()
    pl.when(s < 7)(lambda: arriving(1))
    mcol = pl.ds(PAIR, MIDS)

    for n, b in enumerate((y2, yp, ym, y)):
        more(b, 1)
        along_rest.begin(b)
        ref = wb.at[unit(b, 1 - xh), mcol]
        add(at_unit(b, 1 - xh), 2 * OWN, mid, to=ref)
        pass_on(ref, qx.at[n], rr.at[14 + n], xp)
    along_rest.middle()
    along_near.end(rx.at[0], rr.at[12])
    n_sends = []
    for i in range(1, 16):
        e = (d + i) % 16
        n_sends.append(
            send(
                ni.at[:, pl.ds(base(e), 256)],
                niw.at[pl.ds(al(c * 256 + k * 32, 32), 32)],
                nr.at[i],
                (s, e),
            )
        )


    def one_unit(y_, u):
        return wb.at[unit(y_, xh, 1, u), mcol]

    def mid_sum(y_, u, n):
        return at_unit(y_, xh, u), OWN, mid, qx.at[n, pl.ds(u * OWN, OWN)]

    arrived(qx.at[0], rr.at[14])
    for u, dev in ((0, up), (1, down)):
        add(*mid_sum(y2, u, 0), to=one_unit(y2, u))
        pass_on(one_unit(y2, u), q1.at[u], rr.at[18 + u], dev)
    arrived(qx.at[1], rr.at[15])
    add(*mid_sum(yp, 1, 1), to=one_unit(yp, 1))
    pass_on(one_unit(yp, 1), q23.at[0, 1], rr.at[21], up)
    arrived(qx.at[2], rr.at[16])
    add(*mid_sum(ym, 0, 2), to=one_unit(ym, 0))
    pass_on(one_unit(ym, 0), q23.at[1, 0], rr.at[22], down)
    l_m = [load(first.at[:, half(h)], acc.at[unit(y2, h, 1, 0)], 7 + h) for h in range(2)]
    l_v = [load(second.at[:, half(h)], acc.at[unit(y2, h, 1, 1)], 9 + h) for h in range(2)]
    along_rest.end(rx.at[1], rr.at[13])

    @pl.loop(0, 256 // 32)
    def _(r):
        mo[pl.ds(al(r * 32, 32), 32), :] = jnp.zeros((32, FEAT), BF16)

    arrived(q1.at[0], rr.at[18])
    add(*mid_sum(yp, 0, 1), q1.at[0], to=one_unit(yp, 0))
    pass_on(one_unit(yp, 0), q23.at[0, 0], rr.at[20], up)
    arrived(q1.at[1], rr.at[19])
    add(*mid_sum(ym, 1, 2), q1.at[1], to=one_unit(ym, 1))
    pass_on(one_unit(ym, 1), q23.at[1, 1], rr.at[23], down)

    shift = (d % 4) * 32
    stores, c_sends = [], []

    def zone(n, xh_):
        return (((1 - xh_) * 384, PART), (xh_ * 256, PART + MID))[n]

    def exchanged(n, j):
        width = (PART, PART + MID)[n]
        return pl.ds(n * PAIR + j * width, width)

    def adam(which, n):
        begin, width = zone(n, xh)

        @pl.loop(0, OWN // 16)
        def _(r):
            here = pl.ds(al(r * 16, 16), 16)
            at_m = pl.ds(al(at_unit(y2, which, 0) + r * 16, 16), 16)
            at_v = pl.ds(al(at_unit(y2, which, 1) + r * 16, 16), 16)
            for j in range(2):
                local = pl.ds(al(j * QUART + begin, 128), width)
                cols = pl.ds(al(which * HALF + j * QUART + begin, 128), width)
                if which is c:
                    g = acc[pl.ds(al(at_unit(y, xh, c) + r * 16, 16), 16), local]
                else:
                    g = gx[here, exchanged(n, j)]
                params = mst[here, cols]
                m = FIRST_DECAY * acc[at_m, local] + (1.0 - FIRST_DECAY) * g
                v = SECOND_DECAY * acc[at_v, local] + (1.0 - SECOND_DECAY) * g * g
                acc[at_m, local] = m
                acc[at_v, local] = v
                direction = m / FIRST_CORRECTION / (jnp.sqrt(v / SECOND_CORRECTION) + EPSILON)
                new = params - LEARN_RATE * (direction + WEIGHT_DECAY * params)
                mst[here, cols] = new
                mo[pl.ds(al(shift + r * 16, 16), 16), cols] = new.astype(BF16)

    def product(c_, cols):
        return jnp.dot(
            niw[pl.ds(al(c_ * 256, 256), 256), :],
            mo[pl.ds(0, 256), cols],
            preferred_element_type=F32,
        )

    def slices(n, xh_):
        begin, width = zone(n, xh_)
        return [
            (h, j, pl.ds(al(which * HALF + j * QUART + begin, 128), width))
            for h, which in enumerate((c, 1 - c))
            for j in range(2)
        ]

    def update(n):
        begin, width = zone(n, xh)
        theirs = pl.ds(al(at_unit(y, xh, 1 - c), 32), OWN)
        for j in range(2):
            pass_on(
                acc.at[theirs, pl.ds(al(j * QUART + begin, 128), width)],
                gx.at[:, exchanged(n, j)],
                rr.at[24 + 2 * n + j],
                sib,
            )
        if n == 0:
            for copy in l_m + l_v:
                copy.wait()
            l_ni.wait()
            for i in range(1, 16):
                e = (d - i + 16) % 16
                arrived(niw.at[pl.ds(al((e % 2) * 256 + (e // 2) * 32, 32), 32)], nr.at[i])
        for turn, which in enumerate((c, 1 - c)):
            if turn == 1:
                for j in range(2):
                    arrived(gx.at[:, exchanged(n, j)], rr.at[24 + 2 * n + j])
            adam(which, n)
            for h, j, cols in slices(n, xh):
                if h == turn:
                    gv[pl.ds(0, 256), cols] = product(1 - c, cols).astype(BF16)
                    sem = zr.at[n * 4 + (1 - h) * 2 + j]
                    c_sends.append(send(gv.at[pl.ds(0, 256), cols], cz.at[:, cols], sem, sib))
        for h, j, cols in reversed(slices(n, xh)):
            total = product(c, cols)
            arrived(cz.at[:, cols], zr.at[n * 4 + h * 2 + j])
            gv[pl.ds(256, 256), cols] = (total + cz[:, cols].astype(F32)).astype(BF16)
            for i in range(1, 8):
                e = (k + i) % 8
                c_sends.append(
                    send(
                        gv.at[pl.ds(al(256 + e * 32, 32), 32), cols],
                        cr.at[i, :, cols],
                        cs.at[i, n * 4 + h * 2 + j],
                        (s, e * 2 + c),
                    )
                )

    arrived(qx.at[3], rr.at[17])
    arrived(rx.at[0], rr.at[12])
    add(at_unit(y, xh), 2 * OWN, rest, rx.at[0])
    update(0)
    for u in range(2):
        arrived(q23.at[0, u], rr.at[20 + u])
        arrived(q23.at[1, u], rr.at[22 + u])
        add(*mid_sum(y, u, 3), q23.at[0, u], q23.at[1, u])
    arrived(rx.at[1], rr.at[13])
    add(at_unit(y, xh), 2 * OWN, near, rx.at[1])
    update(1)
    for h in range(2):
        stores.append(load(mst.at[:, half(h)], out_p.at[:, half(h)], 11 + h))
        stores.append(load(acc.at[unit(y2, h, 1, 0)], out_m.at[:, half(h)], 13 + h))
        stores.append(load(acc.at[unit(y2, h, 1, 1)], out_v.at[:, half(h)], 15 + h))
    for n in range(2):
        for i in range(1, 8):
            for h, j, cols in slices(n, (k - i + 8) % 2):
                arrived(cr.at[i, :, cols], cs.at[i, n * 4 + h * 2 + j])

    @pl.loop(0, 2)
    def _(r):
        here = pl.ds(al(r * 16, 16), 16)
        for q in range(4):
            cols = pl.ds(q * QUART, QUART)
            total = gv[pl.ds(al(256 + k * 32 + r * 16, 16), 16), cols].astype(F32)
            for i in range(1, 8):
                total += cr[i, here, cols].astype(F32)
            res[here, cols] = total.astype(BF16)

    stores.append(load(res, out_c, 17))
    for copy in stores:
        copy.wait()
    for copy in n_sends + r_sends + c_sends:
        copy.wait_send()

    @pl.when(s > 0)
    def _():
        for copy in p_sends:
            copy.wait_send()


def settle_kernel(*refs):
    count = len(refs) // 4
    sources, targets, held, sems = (refs[i * count : (i + 1) * count] for i in range(4))
    taken, given = [], []
    for source, target, middle, sem in zip(sources, targets, held, sems):
        height = source.shape[0] // 4 if source.shape[0] == OWN else source.shape[0]
        for i in range(source.shape[0] // height):
            rows = pl.ds(i * height, height)
            taken.append(pltpu.make_async_copy(source.at[rows], middle.at[rows], sem.at[0, i]))
            given.append(pltpu.make_async_copy(middle.at[rows], target.at[rows], sem.at[1, i]))
    for copy in taken:
        copy.start()
    for copy, onward in zip(taken, given):
        copy.wait()
        onward.start()
    for copy in given:
        copy.wait()


def settle(*values):
    anywhere = pl.BlockSpec(memory_space=pl.ANY)
    return pl.pallas_call(
        settle_kernel,
        out_shape=tuple(jax.ShapeDtypeStruct(v.shape, v.dtype) for v in values),
        in_specs=[anywhere] * len(values),
        out_specs=[anywhere] * len(values),
        scratch_shapes=[pltpu.VMEM(v.shape, v.dtype) for v in values]
        + [pltpu.SemaphoreType.DMA((2, 4)) for _ in values],
        name="settle",
    )(*values)


def step(master, first, second, xo, xa, grads, wo, wa, ni):
    vm = pltpu.VMEM
    dma = pltpu.SemaphoreType.DMA
    anywhere = pl.BlockSpec(memory_space=pl.ANY)
    shape = jax.ShapeDtypeStruct
    flat = (ROWS, FEAT)
    new = pl.pallas_call(
        kernel,
        out_shape=(
            shape((OWN, FEAT), F32),
            shape((OWN, FEAT), F32),
            shape((OWN, FEAT), F32),
            shape((32, FEAT), BF16),
        ),
        in_specs=[anywhere] * 9,
        out_specs=[anywhere] * 4,
        scratch_shapes=[
            vm((FEAT, FEAT), BF16),
            vm(flat, BF16),
            vm((ROWS, HALF), BF16),
            vm((2, ROWS, FEAT), BF16),
            vm((2, ROWS, FEAT), BF16),
            vm((FEAT, HALF), F32),
            vm(flat, BF16),
            vm((TOK, FEAT), jnp.int32),
            vm((2, TOK, HALF), jnp.int32),
            vm((OWN, FEAT), F32),
            vm((4, ROWS, QUART), BF16),
            vm((2, 2, ROWS, QUART), BF16),
            vm((512, 256), BF16),
            vm((2, 2 * OWN, PAIR), BF16),
            vm((2, 2, 2 * OWN, PAIR), BF16),
            vm((2, 2 * OWN, PAIR), BF16),
            vm((2, 2, 2 * OWN, PAIR), BF16),
            vm((2, 2 * OWN, PAIR), BF16),
            vm((4, 2 * OWN, MIDS), BF16),
            vm((2, OWN, MIDS), BF16),
            vm((2, 2, OWN, MIDS), BF16),
            vm((OWN, HALF), F32),
            vm((256, FEAT), BF16),
            vm((8, 32, FEAT), BF16),
            vm((32, FEAT), BF16),
            dma((18,)),
            dma((224,)),
            dma((9,)),
            dma((10,)),
            dma((4,)),
            dma((16,)),
            dma((2, 2, 2, 2)),
            dma((28,)),
            dma((8,)),
            dma((8, 8)),
        ],
        compiler_params=pltpu.CompilerParams(
            collective_id=0, has_side_effects=True, vmem_limit_bytes=67043328
        ),
        name="section_step",
    )(
        master[0],
        first[0],
        second[0],
        xo[0].reshape(flat),
        xa[0].reshape(flat),
        grads[0].reshape(flat),
        wo[0],
        wa[0],
        ni[0],
    )
    return tuple(value[None] for value in settle(*new))


def solution(mesh):
    row = P("section", "dp", None)
    deep = P("section", None, "dp", None)
    return jax.shard_map(
        step,
        mesh=mesh,
        in_specs=(row, row, row, deep, deep, deep, row, row, row),
        out_specs=(row, row, row, row),
        check_vma=False,
    )
```

```python
import jax
import jax.numpy as jnp
from jax import lax
from jax.experimental import pallas as pl
from jax.experimental.pallas import tpu as pltpu
from jax.sharding import PartitionSpec as P

LEAK_RATE = 0.5
LEARN_RATE = 0.002
FIRST_DECAY = 0.9
SECOND_DECAY = 0.95
EPSILON = 1e-08
WEIGHT_DECAY = 0.1
FIRST_CORRECTION = 1.0 - 0.9**10
SECOND_CORRECTION = 1.0 - 0.95**10

MESH = pl.DeviceIdType.MESH
F32, BF16 = jnp.float32, jnp.bfloat16
FEAT, HALF, QUART, OWN = 2560, 1280, 640, 160
ROWS, TOK, STEPS = 512, 128, 4
PART, MID = 256, 128
PAIR, MIDS = 2 * PART, 2 * MID


def al(value, by):
    return pl.multiple_of(value, by)


def kernel(
    master, first, second, xo, xa, grads, wo, wa, ni,
    out_p, out_m, out_v, out_c,
    wb, mo, mos, xov, xav, acc, gv, wov, wav, mst, outb, rcv, niw,
    n1, n23, r1, r23, rx, qx, q1, q23, gx, cz, cr, res,
    loc, snd, wr, ws, xs, nr, pr, rr, zr, cs,
):
    s, d = lax.axis_index("section"), lax.axis_index("dp")
    y, xh, c, k = d // 4, (d // 2) % 2, d % 2, d // 2
    yp, ym, y2 = (y + 1) % 4, (y + 3) % 4, (y + 2) % 4

    def index(y_, xh_, c_):
        return (y_ * 2 + xh_) * 2 + c_

    sib, xp = (s, index(y, xh, 1 - c)), (s, index(y, 1 - xh, c))
    up, down = (s, index(yp, xh, c)), (s, index(ym, xh, c))
    used = [0]

    def send(src, dst, sem, dev):
        copy = pltpu.make_async_remote_copy(
            src_ref=src, dst_ref=dst, send_sem=snd.at[used[0]], recv_sem=sem,
            device_id=dev, device_id_type=MESH,
        )
        used[0] += 1
        copy.start()
        return copy

    def arrived(dst, sem):
        pltpu.make_async_remote_copy(
            src_ref=dst, dst_ref=dst, send_sem=snd.at[0], recv_sem=sem,
            device_id=sib, device_id_type=MESH,
        ).wait_recv()

    def load(src, dst, i):
        copy = pltpu.make_async_copy(src, dst, loc.at[i])
        copy.start()
        return copy

    def owner(y_, xh_, c_, part=0, rows=OWN):
        return wb.at[pl.ds(al(index(y_, xh_, c_) * OWN + part, 16), rows)]

    def half(which):
        return pl.ds(al(which * HALF, 128), HALF)

    l_mst = load(master, mst, 0)
    l_g = load(grads, gv, 1)
    l_wo = load(wo, wov, 2)
    l_xo = load(xo, xov.at[c], 3)
    l_xa = load(xa, xav.at[c], 4)
    l_wa = load(wa.at[:, half(c)], wav.at[c], 5)

    def base(e):
        return al(e * OWN - (e % 4) * 32, 128)

    l_ni = load(
        ni.at[:, pl.ds(base(d), 256)], niw.at[pl.ds(al(c * 256 + k * 32, 32), 32)], 6
    )

    barrier = pltpu.get_barrier_semaphore()
    for dev in (up, down, xp, sib):
        pl.semaphore_signal(barrier, inc=1, device_id=dev, device_id_type=MESH)

    @pl.when(s > 0)
    def _():
        for h in range(2):
            pl.semaphore_signal(barrier, inc=1, device_id=(s - 1, k * 2 + h), device_id_type=MESH)

    @pl.when(s < 7)
    def _():
        for h in range(2):
            pl.semaphore_signal(barrier, inc=1, device_id=(s + 1, k * 2 + h), device_id_type=MESH)

    l_mst.wait()

    @pl.loop(0, OWN // 16)
    def _(r):
        wb[pl.ds(al(d * OWN + r * 16, 16), 16), :] = mst[pl.ds(al(r * 16, 16), 16), :].astype(BF16)

    pl.semaphore_wait(barrier, 4 + 2 * jnp.minimum(s, 1) + 2 * jnp.minimum(7 - s, 1))

    mine = owner(y, xh, c)
    w_sends = [
        send(mine, mine, wr.at[0], xp),
        send(mine, mine, wr.at[1], up),
        send(mine, mine, wr.at[2], down),
        send(mine, mine, ws.at[0], sib),
    ]
    x_sends = [
        send(xo, xov.at[c], xs.at[0], sib),
        send(wa.at[:, half(1 - c)], wav.at[c], xs.at[1], sib),
    ]
    l_g.wait()
    l_wo.wait()

    @pl.loop(0, TOK // 16)
    def _(r):
        for q in range(4):
            cols = pl.ds(q * QUART, QUART)
            bits = wov[pl.ds(al(r * 16, 16), 16), cols]
            carry = jnp.zeros((16, QUART), F32)
            for t in reversed(range(STEPS)):
                rows = pl.ds(al(t * TOK + r * 16, 16), 16)
                window = ((bits >> t) & 1).astype(F32)
                carry = window * gv[rows, cols].astype(F32) + LEAK_RATE * carry
                mo[rows, cols] = carry.astype(BF16)

    x_sends.append(send(mo.at[:, half(1 - c)], mos, xs.at[3], sib))
    x_sends.append(send(xa, xav.at[c], xs.at[2], sib))

    p_sends = []

    parts = ((xh * 384, 256), ((1 - xh) * 256, 384))

    def outgoing(b, n, part):
        begin, width = parts[part]
        cols = pl.ds(al(begin, 128), width)
        wide = pl.ds(al(b * QUART + begin, 128), width)
        for h in (1, 0):
            rows = pl.ds(h * 256, 256)
            through = lax.dot_general(
                mo[rows, :], wb[wide, :], (((1,), (1,)), ((), ())), preferred_element_type=F32
            )
            outb[n, rows, cols] = (gv[rows, wide].astype(F32) + through).astype(BF16)
            copy = pltpu.make_async_remote_copy(
                src_ref=outb.at[n, rows, cols],
                dst_ref=rcv.at[c, b % 2, rows, cols],
                send_sem=snd.at[used[0]],
                recv_sem=pr.at[c, b % 2, part, h],
                device_id=(s - 1, k * 2 + b // 2),
                device_id_type=MESH,
            )
            used[0] += 1
            p_sends.append(copy)
            pl.when(s > 0)(copy.start)

    def relay(kind, piece, *targets):
        arrived(piece, wr.at[kind])
        for region, sem, dev in targets:
            w_sends.append(send(region, region, sem, dev))

    arrived(owner(y, xh, 1 - c), ws.at[0])
    outgoing(y, 0, 0)
    piece = owner(ym, xh, c)
    relay(1, piece, (owner(ym, xh, c, 0, 80), wr.at[5], up))
    piece = owner(yp, xh, c)
    relay(2, piece, (owner(yp, xh, c, 80, 80), wr.at[6], down))
    piece = owner(y, 1 - xh, c)
    relay(0, piece, (piece, ws.at[1], sib), (piece, wr.at[3], up), (piece, wr.at[4], down))
    for piece, i in ((owner(ym, xh, c), 2), (owner(yp, xh, c), 3)):
        w_sends.append(send(piece, piece, ws.at[i], sib))
    arrived(owner(y, 1 - xh, 1 - c), ws.at[1])
    outgoing(y, 0, 1)
    arrived(owner(ym, xh, 1 - c), ws.at[2])
    outgoing(ym, 1, 0)
    arrived(owner(yp, xh, 1 - c), ws.at[3])
    outgoing(yp, 2, 0)

    across = (((0,), (0,)), ((), ()))
    l_xo.wait()
    arrived(xov.at[1 - c], xs.at[0])
    arrived(mos, xs.at[3])

    @pl.loop(0, 4)
    def _(b):
        rows = pl.ds(al(b * QUART, 128), QUART)
        for j in range(2):
            acc[rows, pl.ds(j * QUART, QUART)] = lax.dot_general(
                xov[c, :, rows],
                mo[:, pl.ds(al(c * HALF + j * QUART, 128), QUART)],
                across,
                preferred_element_type=F32,
            ) + lax.dot_general(
                xov[1 - c, :, rows],
                mos[:, pl.ds(j * QUART, QUART)],
                across,
                preferred_element_type=F32,
            )

    def far_block(xh_, n):
        for i in range(2):
            piece = owner(y2, xh_, c, 80 * i, 80)
            relay(5 + 2 * n + i, piece, (piece, ws.at[6 + 2 * n + i], sib))
        for i in range(2):
            arrived(owner(y2, xh_, 1 - c, 80 * i, 80), ws.at[6 + 2 * n + i])
        outgoing(y2, 3, n)

    far_block(xh, 0)
    piece = owner(ym, 1 - xh, c)
    relay(3, piece, (owner(ym, 1 - xh, c, 0, 80), wr.at[7], up), (piece, ws.at[4], sib))
    piece = owner(yp, 1 - xh, c)
    relay(4, piece, (owner(yp, 1 - xh, c, 80, 80), wr.at[8], down), (piece, ws.at[5], sib))
    arrived(owner(ym, 1 - xh, 1 - c), ws.at[4])
    outgoing(ym, 1, 1)
    arrived(owner(yp, 1 - xh, 1 - c), ws.at[5])
    outgoing(yp, 2, 1)

    l_xa.wait()
    arrived(xav.at[1 - c], xs.at[2])
    l_wa.wait()
    arrived(wav.at[1 - c], xs.at[1])

    def arriving(part):
        begin, width = parts[part]
        cols = pl.ds(al(begin, 128), width)
        for j in range(2):
            for cc in range(2):
                for h in (1, 0):
                    arrived(rcv.at[cc, j, pl.ds(h * 256, 256), cols], pr.at[cc, j, part, h])

                @pl.loop(0, TOK // 16)
                def _(r, cc=cc, j=j):
                    here = pl.ds(al(r * 16, 16), 16)
                    bits = wav[cc, here, pl.ds(al(j * QUART + begin, 128), width)]
                    carry = jnp.zeros((16, width), F32)
                    for t in reversed(range(STEPS)):
                        rows = pl.ds(al(t * TOK + r * 16, 16), 16)
                        window = ((bits >> t) & 1).astype(F32)
                        carry = window * rcv[cc, j, rows, cols].astype(F32) + LEAK_RATE * carry
                        rcv[cc, j, rows, cols] = carry.astype(BF16)

    def more(b, part):
        begin, width = parts[part]
        rows = pl.ds(al(b * QUART, 128), QUART)
        cols = pl.ds(al(begin, 128), width)

        @pl.when(s < 7)
        def _():
            for j in range(2):
                acc[rows, pl.ds(al(j * QUART + begin, 128), width)] += lax.dot_general(
                    xav[0, :, rows], rcv[0, j, :, cols], across, preferred_element_type=F32
                ) + lax.dot_general(
                    xav[1, :, rows], rcv[1, j, :, cols], across, preferred_element_type=F32
                )

    near, rest, mid = (xh * 384, PART), ((1 - xh) * 384, PART), (PART, MID)
    r_sends = []

    def at_unit(y_, xh_, c_=0):
        return index(y_, xh_, c_) * OWN

    def unit(y_, xh_, n=2, first_=0):
        return pl.ds(al(at_unit(y_, xh_, first_), 32), n * OWN)

    def add(start, count, group, *terms, to=None):
        begin, width = group
        height = 32

        @pl.loop(0, count // height)
        def _(r):
            rows = pl.ds(al(start + r * height, 32), height)
            here = pl.ds(al(r * height, 32), height)
            for j in range(2):
                cols = pl.ds(al(j * QUART + begin, 128), width)
                side = pl.ds(j * width, width)
                total = acc[rows, cols]
                for term in terms:
                    total += term[here, side].astype(F32)
                if to is None:
                    acc[rows, cols] = total
                else:
                    to[here, side] = total.astype(BF16)

    def pass_on(src, dst, sem, dev):
        r_sends.append(send(src, dst, sem, dev))

    class AlongY:
        def __init__(self, group, place, one, two, sems):
            self.group, self.place, self.one, self.two, self.sems = group, place, one, two, sems

        def begin(self, b):
            for xh_ in range(2):
                keep = (b is yp and xh_ == 0) or (b is ym and xh_ == 1) or b is y
                if keep:
                    continue
                ref = self.place(b, xh_)
                add(at_unit(b, xh_), 2 * OWN, self.group, to=ref)
                if b is y2:
                    pass_on(ref, self.one.at[xh_], rr.at[self.sems + xh_], (up, down)[xh_])
                elif b is yp:
                    pass_on(ref, self.two.at[0, 1], rr.at[self.sems + 3], up)
                else:
                    pass_on(ref, self.two.at[1, 0], rr.at[self.sems + 4], down)

        def middle(self):
            for xh_, b, dev, sem in ((0, yp, up, 2), (1, ym, down, 5)):
                arrived(self.one.at[xh_], rr.at[self.sems + xh_])
                ref = self.place(b, xh_)
                add(at_unit(b, xh_), 2 * OWN, self.group, self.one.at[xh_], to=ref)
                pass_on(ref, self.two.at[xh_, xh_], rr.at[self.sems + sem], dev)

        def end(self, there, sem):
            for i, h, sem_ in ((0, 1, 3), (1, 0, 4), (0, 0, 2), (1, 1, 5)):
                arrived(self.two.at[i, h], rr.at[self.sems + sem_])
            other = self.place(y, 1 - xh)
            add(
                at_unit(y, 1 - xh), 2 * OWN, self.group,
                self.two.at[0, 1 - xh], self.two.at[1, 1 - xh], to=other,
            )
            pass_on(other, there, sem, xp)
            add(at_unit(y, xh), 2 * OWN, self.group, self.two.at[0, xh], self.two.at[1, xh])

    def near_place(b, xh_):
        chip = b * 2 + xh_
        return xov.at[chip // 5, pl.ds(0, 2 * OWN), pl.ds(al((chip % 5) * PAIR, 128), PAIR)]

    def rest_place(b, xh_):
        return wb.at[unit(b, xh_), pl.ds(0, PAIR)]

    along_near = AlongY(near, near_place, n1, n23, 0)
    along_rest = AlongY(rest, rest_place, r1, r23, 6)

    pl.when(s < 7)(lambda: arriving(0))
    for b in (y2, yp, ym, y):
        more(b, 0)
        along_near.begin(b)

    far_block(1 - xh, 1)
    along_near.middle()
    for copy in w_sends + x_sends:
        copy.wait_send()
    pl.when(s < 7)(lambda: arriving(1))
    mcol = pl.ds(PAIR, MIDS)

    for n, b in enumerate((y2, yp, ym, y)):
        more(b, 1)
        along_rest.begin(b)
        ref = wb.at[unit(b, 1 - xh), mcol]
        add(at_unit(b, 1 - xh), 2 * OWN, mid, to=ref)
        pass_on(ref, qx.at[n], rr.at[14 + n], xp)
    along_rest.middle()
    along_near.end(rx.at[0], rr.at[12])
    n_sends = []
    for i in range(1, 16):
        e = (d + i) % 16
        n_sends.append(
            send(
                ni.at[:, pl.ds(base(e), 256)],
                niw.at[pl.ds(al(c * 256 + k * 32, 32), 32)],
                nr.at[i],
                (s, e),
            )
        )


    def one_unit(y_, u):
        return wb.at[unit(y_, xh, 1, u), mcol]

    def mid_sum(y_, u, n):
        return at_unit(y_, xh, u), OWN, mid, qx.at[n, pl.ds(u * OWN, OWN)]

    arrived(qx.at[0], rr.at[14])
    for u, dev in ((0, up), (1, down)):
        add(*mid_sum(y2, u, 0), to=one_unit(y2, u))
        pass_on(one_unit(y2, u), q1.at[u], rr.at[18 + u], dev)
    arrived(qx.at[1], rr.at[15])
    add(*mid_sum(yp, 1, 1), to=one_unit(yp, 1))
    pass_on(one_unit(yp, 1), q23.at[0, 1], rr.at[21], up)
    arrived(qx.at[2], rr.at[16])
    add(*mid_sum(ym, 0, 2), to=one_unit(ym, 0))
    pass_on(one_unit(ym, 0), q23.at[1, 0], rr.at[22], down)
    l_m = [load(first.at[:, half(h)], acc.at[unit(y2, h, 1, 0)], 7 + h) for h in range(2)]
    l_v = [load(second.at[:, half(h)], acc.at[unit(y2, h, 1, 1)], 9 + h) for h in range(2)]
    along_rest.end(rx.at[1], rr.at[13])

    @pl.loop(0, 256 // 32)
    def _(r):
        mo[pl.ds(al(r * 32, 32), 32), :] = jnp.zeros((32, FEAT), BF16)

    arrived(q1.at[0], rr.at[18])
    add(*mid_sum(yp, 0, 1), q1.at[0], to=one_unit(yp, 0))
    pass_on(one_unit(yp, 0), q23.at[0, 0], rr.at[20], up)
    arrived(q1.at[1], rr.at[19])
    add(*mid_sum(ym, 1, 2), q1.at[1], to=one_unit(ym, 1))
    pass_on(one_unit(ym, 1), q23.at[1, 1], rr.at[23], down)

    shift = (d % 4) * 32
    stores, c_sends = [], []

    def zone(n, xh_):
        return (((1 - xh_) * 384, PART), (xh_ * 256, PART + MID))[n]

    def exchanged(n, j):
        width = (PART, PART + MID)[n]
        return pl.ds(n * PAIR + j * width, width)

    def adam(which, n):
        begin, width = zone(n, xh)

        @pl.loop(0, OWN // 16)
        def _(r):
            here = pl.ds(al(r * 16, 16), 16)
            at_m = pl.ds(al(at_unit(y2, which, 0) + r * 16, 16), 16)
            at_v = pl.ds(al(at_unit(y2, which, 1) + r * 16, 16), 16)
            for j in range(2):
                local = pl.ds(al(j * QUART + begin, 128), width)
                cols = pl.ds(al(which * HALF + j * QUART + begin, 128), width)
                if which is c:
                    g = acc[pl.ds(al(at_unit(y, xh, c) + r * 16, 16), 16), local]
                else:
                    g = gx[here, exchanged(n, j)]
                params = mst[here, cols]
                m = FIRST_DECAY * acc[at_m, local] + (1.0 - FIRST_DECAY) * g
                v = SECOND_DECAY * acc[at_v, local] + (1.0 - SECOND_DECAY) * g * g
                acc[at_m, local] = m
                acc[at_v, local] = v
                direction = m / FIRST_CORRECTION / (jnp.sqrt(v / SECOND_CORRECTION) + EPSILON)
                new = params - LEARN_RATE * (direction + WEIGHT_DECAY * params)
                mst[here, cols] = new
                mo[pl.ds(al(shift + r * 16, 16), 16), cols] = new.astype(BF16)

    def product(c_, cols):
        return jnp.dot(
            niw[pl.ds(al(c_ * 256, 256), 256), :],
            mo[pl.ds(0, 256), cols],
            preferred_element_type=F32,
        )

    def slices(n, xh_):
        begin, width = zone(n, xh_)
        return [
            (h, j, pl.ds(al(which * HALF + j * QUART + begin, 128), width))
            for h, which in enumerate((c, 1 - c))
            for j in range(2)
        ]

    def update(n):
        begin, width = zone(n, xh)
        theirs = pl.ds(al(at_unit(y, xh, 1 - c), 32), OWN)
        for j in range(2):
            pass_on(
                acc.at[theirs, pl.ds(al(j * QUART + begin, 128), width)],
                gx.at[:, exchanged(n, j)],
                rr.at[24 + 2 * n + j],
                sib,
            )
        if n == 0:
            for copy in l_m + l_v:
                copy.wait()
            l_ni.wait()
            for i in range(1, 16):
                e = (d - i + 16) % 16
                arrived(niw.at[pl.ds(al((e % 2) * 256 + (e // 2) * 32, 32), 32)], nr.at[i])
        for turn, which in enumerate((c, 1 - c)):
            if turn == 1:
                for j in range(2):
                    arrived(gx.at[:, exchanged(n, j)], rr.at[24 + 2 * n + j])
            adam(which, n)
            for h, j, cols in slices(n, xh):
                if h == turn:
                    gv[pl.ds(0, 256), cols] = product(1 - c, cols).astype(BF16)
                    sem = zr.at[n * 4 + (1 - h) * 2 + j]
                    c_sends.append(send(gv.at[pl.ds(0, 256), cols], cz.at[:, cols], sem, sib))
        for h, j, cols in reversed(slices(n, xh)):
            total = product(c, cols)
            arrived(cz.at[:, cols], zr.at[n * 4 + h * 2 + j])
            gv[pl.ds(256, 256), cols] = (total + cz[:, cols].astype(F32)).astype(BF16)
            for i in range(1, 8):
                e = (k + i) % 8
                c_sends.append(
                    send(
                        gv.at[pl.ds(al(256 + e * 32, 32), 32), cols],
                        cr.at[i, :, cols],
                        cs.at[i, n * 4 + h * 2 + j],
                        (s, e * 2 + c),
                    )
                )

    arrived(qx.at[3], rr.at[17])
    arrived(rx.at[0], rr.at[12])
    add(at_unit(y, xh), 2 * OWN, rest, rx.at[0])
    update(0)
    for u in range(2):
        arrived(q23.at[0, u], rr.at[20 + u])
        arrived(q23.at[1, u], rr.at[22 + u])
        add(*mid_sum(y, u, 3), q23.at[0, u], q23.at[1, u])
    arrived(rx.at[1], rr.at[13])
    add(at_unit(y, xh), 2 * OWN, near, rx.at[1])
    update(1)
    for h in range(2):
        stores.append(load(mst.at[:, half(h)], out_p.at[:, half(h)], 11 + h))
        stores.append(load(acc.at[unit(y2, h, 1, 0)], out_m.at[:, half(h)], 13 + h))
        stores.append(load(acc.at[unit(y2, h, 1, 1)], out_v.at[:, half(h)], 15 + h))
    for n in range(2):
        for i in range(1, 8):
            for h, j, cols in slices(n, (k - i + 8) % 2):
                arrived(cr.at[i, :, cols], cs.at[i, n * 4 + h * 2 + j])

    @pl.loop(0, 2)
    def _(r):
        here = pl.ds(al(r * 16, 16), 16)
        for q in range(4):
            cols = pl.ds(q * QUART, QUART)
            total = gv[pl.ds(al(256 + k * 32 + r * 16, 16), 16), cols].astype(F32)
            for i in range(1, 8):
                total += cr[i, here, cols].astype(F32)
            res[here, cols] = total.astype(BF16)

    stores.append(load(res, out_c, 17))
    for copy in stores:
        copy.wait()
    for copy in n_sends + r_sends + c_sends:
        copy.wait_send()

    @pl.when(s > 0)
    def _():
        for copy in p_sends:
            copy.wait_send()


def settle_kernel(*refs):
    count = len(refs) // 4
    sources, targets, held, sems = (refs[i * count : (i + 1) * count] for i in range(4))
    taken, given = [], []
    for source, target, middle, sem in zip(sources, targets, held, sems):
        height = source.shape[0] // 4 if source.shape[0] == OWN else source.shape[0]
        for i in range(source.shape[0] // height):
            rows = pl.ds(i * height, height)
            taken.append(pltpu.make_async_copy(source.at[rows], middle.at[rows], sem.at[0, i]))
            given.append(pltpu.make_async_copy(middle.at[rows], target.at[rows], sem.at[1, i]))
    for copy in taken:
        copy.start()
    for copy, onward in zip(taken, given):
        copy.wait()
        onward.start()
    for copy in given:
        copy.wait()


def settle(*values):
    anywhere = pl.BlockSpec(memory_space=pl.ANY)
    return pl.pallas_call(
        settle_kernel,
        out_shape=tuple(jax.ShapeDtypeStruct(v.shape, v.dtype) for v in values),
        in_specs=[anywhere] * len(values),
        out_specs=[anywhere] * len(values),
        scratch_shapes=[pltpu.VMEM(v.shape, v.dtype) for v in values]
        + [pltpu.SemaphoreType.DMA((2, 4)) for _ in values],
        name="settle",
    )(*values)


def step(master, first, second, xo, xa, grads, wo, wa, ni):
    vm = pltpu.VMEM
    dma = pltpu.SemaphoreType.DMA
    anywhere = pl.BlockSpec(memory_space=pl.ANY)
    shape = jax.ShapeDtypeStruct
    flat = (ROWS, FEAT)
    new = pl.pallas_call(
        kernel,
        out_shape=(
            shape((OWN, FEAT), F32),
            shape((OWN, FEAT), F32),
            shape((OWN, FEAT), F32),
            shape((32, FEAT), BF16),
        ),
        in_specs=[anywhere] * 9,
        out_specs=[anywhere] * 4,
        scratch_shapes=[
            vm((FEAT, FEAT), BF16),
            vm(flat, BF16),
            vm((ROWS, HALF), BF16),
            vm((2, ROWS, FEAT), BF16),
            vm((2, ROWS, FEAT), BF16),
            vm((FEAT, HALF), F32),
            vm(flat, BF16),
            vm((TOK, FEAT), jnp.int32),
            vm((2, TOK, HALF), jnp.int32),
            vm((OWN, FEAT), F32),
            vm((4, ROWS, QUART), BF16),
            vm((2, 2, ROWS, QUART), BF16),
            vm((512, 256), BF16),
            vm((2, 2 * OWN, PAIR), BF16),
            vm((2, 2, 2 * OWN, PAIR), BF16),
            vm((2, 2 * OWN, PAIR), BF16),
            vm((2, 2, 2 * OWN, PAIR), BF16),
            vm((2, 2 * OWN, PAIR), BF16),
            vm((4, 2 * OWN, MIDS), BF16),
            vm((2, OWN, MIDS), BF16),
            vm((2, 2, OWN, MIDS), BF16),
            vm((OWN, HALF), F32),
            vm((256, FEAT), BF16),
            vm((8, 32, FEAT), BF16),
            vm((32, FEAT), BF16),
            dma((18,)),
            dma((224,)),
            dma((9,)),
            dma((10,)),
            dma((4,)),
            dma((16,)),
            dma((2, 2, 2, 2)),
            dma((28,)),
            dma((8,)),
            dma((8, 8)),
        ],
        compiler_params=pltpu.CompilerParams(
            collective_id=0, has_side_effects=True, vmem_limit_bytes=67043328
        ),
        name="section_step",
    )(
        master[0],
        first[0],
        second[0],
        xo[0].reshape(flat),
        xa[0].reshape(flat),
        grads[0].reshape(flat),
        wo[0],
        wa[0],
        ni[0],
    )
    return tuple(value[None] for value in settle(*new))


def solution(mesh):
    row = P("section", "dp", None)
    deep = P("section", None, "dp", None)
    return jax.shard_map(
        step,
        mesh=mesh,
        in_specs=(row, row, row, deep, deep, deep, row, row, row),
        out_specs=(row, row, row, row),
        check_vma=False,
    )
```
